128 devices in a mesh: gx: 16 (over x, y), gy: 8 (over z, core).
Axes of the slice: x: 4, y: 4, z: 4, core: 2. Of those that a mesh axis runs over, the one named last changes fastest.
Arguments:
- tensor: float32 [256, 512, 1024], P('gx', None, 'gy'), may hold values from -80 to 80
- start_basis: float32 [512, 384], replicated, may hold values from -6 to 6
Outputs:
- core: float32 [256, 384, 1024], P('gx', 'gy')
The draws below stay inside these ranges and needn't reach their ends.
All inputs are finite; a program needn't handle non-finite values.
Results may differ from the reference program's by a relative error of at most 0.00019.
Values sent between devices are 32-bit elements; how exact they have to be, the bound alone decides.
A program may use at most 512 MiB of HBM per device.

```python
import jax
import jax.numpy as jnp
from jax import lax

I1 = 512
R1 = 384
I2 = 1024
ITERS = 2
I3 = 256


def draw_tensor(key, part):
    key_values = jax.random.fold_in(key, 11)
    key_rows = jax.random.fold_in(key, 12)
    key_columns = jax.random.fold_in(key, 13)
    key_slabs = jax.random.fold_in(key, 14)
    values = jnp.clip(jax.random.normal(key_values, (I3, I1, I2), jnp.float32), -5.0, 5.0)
    row_scale = jnp.exp(jax.random.uniform(key_rows, (I1,), jnp.float32, 0.0, 0.9))
    column_scale = jnp.exp(jax.random.uniform(key_columns, (I2,), jnp.float32, -0.35, 0.35))
    slab_scale = jnp.exp(jax.random.uniform(key_slabs, (I3,), jnp.float32, -0.35, 0.35))
    slab_trend = jnp.exp(0.275 * jnp.arange(I3, dtype=jnp.float32) / max(I3 - 1, 1))
    column_trend = jnp.exp(0.275 * jnp.arange(I2, dtype=jnp.float32) / max(I2 - 1, 1))
    slab_factor = (slab_scale * slab_trend)[:, None, None]
    column_factor = (column_scale * column_trend)[None, None, :]
    return values * row_scale[None, :, None] * slab_factor * column_factor


def normal_values(stream_key, dims, spread, reach, kind=jnp.bfloat16):
    return jnp.clip(spread * jax.random.normal(stream_key, dims, jnp.float32), -reach, reach).astype(kind)


def setup_inputs(seed: int = 0) -> dict:
    key_of = jax.random.split(jax.random.key(seed), 3)
    return {
        "tensor": draw_tensor(jax.random.fold_in(key_of[2], 71), 0),
        "start_basis": normal_values(key_of[1], (I1, R1), 1.0, 6.0, jnp.float32),
    }


def orthonormal(product):
    product_gram = jnp.dot(product.T.astype(jnp.float32), product.astype(jnp.float32), precision=lax.Precision.HIGHEST, preferred_element_type=jnp.float32)
    lower = jnp.linalg.cholesky(product_gram)
    return jax.scipy.linalg.solve_triangular(lower, product.T, lower=True).T

def reference(tensor, start_basis):
    gram = lax.dot_general(tensor.astype(jnp.float32), tensor.astype(jnp.float32), (((0, 2), (0, 2)), ((), ())), precision=lax.Precision.HIGHEST, preferred_element_type=jnp.float32)
    basis = start_basis
    for sweep in range(ITERS):
        basis = orthonormal(jnp.dot(gram.astype(jnp.float32), basis.astype(jnp.float32), precision=lax.Precision.HIGHEST, preferred_element_type=jnp.float32))
    core = jnp.einsum('ar,kac->krc', basis.astype(jnp.float32), tensor.astype(jnp.float32), precision=lax.Precision.HIGHEST, preferred_element_type=jnp.float32)
    return core
```

```python
import jax
import jax.numpy as jnp
from jax import lax
from jax.experimental import pallas as pl
from jax.experimental.pallas import tpu as pltpu
from jax.sharding import PartitionSpec as P
HI = lax.Precision.HIGHEST
def mm(a, b, ca=1, cb=0):
    return lax.dot_general(a, b, (((ca,), (cb,)), ((), ())), precision=HI, preferred_element_type=jnp.float32)

def rep(x):
    return jnp.broadcast_to(x, (8, 128))

def chol_inv(D):
    A = list(D)
    row = lax.broadcasted_iota(jnp.int32, (8, 128), 0)
    lane = lax.broadcasted_iota(jnp.int32, (8, 128), 1)
    Z = [jnp.where(lane == row + 8 * g, 1.0, 0.0).astype(jnp.float32) for g in range(16)]
    out = []
    for p in range(16):
        c = 8 * p
        S = [[rep(A[p][i:i+1, c+j:c+j+1]) for j in range(i+1)] for i in range(8)]
        V = [rep(A[p][i:i+1, :]) for i in range(8)]
        U = [rep(Z[p][i:i+1, :]) for i in range(8)]
        L = [[None]*8 for _ in range(8)]
        r = [None]*8
        for j in range(8):
            r[j] = lax.rsqrt(S[j][j])
            for i in range(j+1, 8):
                L[i][j] = S[i][j] * r[j]
            for i in range(j+1, 8):
                for k in range(j+1, i+1):
                    S[i][k] = S[i][k] - L[i][j] * L[k][j]
            V[j] = V[j] * r[j]
            U[j] = U[j] * r[j]
            for i in range(j+1, 8):
                V[i] = V[i] - L[i][j] * V[j]
                U[i] = U[i] - L[i][j] * U[j]
        o = U[0]
        for i in range(1, 8):
            o = jnp.where(row == i, U[i], o)
        out.append(o)
        if p == 15:
            break
        F = list(V); FU = list(U)
        for j in range(7, -1, -1):
            F[j] = F[j] * r[j]
            FU[j] = FU[j] * r[j]
            for i in range(j):
                F[i] = F[i] - L[j][i] * F[j]
                FU[i] = FU[i] - L[j][i] * FU[j]
        for g in range(p+1, 16):
            X = [jnp.broadcast_to(A[g][:, c+j:c+j+1], (8, 128)) for j in range(8)]
            def acc(Y, F):
                t = [X[j]*F[j] for j in range(8)]
                t = [t[0]+t[1], t[2]+t[3], t[4]+t[5], t[6]+t[7]]
                return Y - ((t[0]+t[1]) + (t[2]+t[3]))
            Z[g] = acc(Z[g], FU)
            A[g] = acc(A[g], F)
    return out

def qr_kernel(g_ref, b_ref, o_ref, pt, a, li):
    pt[...] = mm(b_ref[...], g_ref[...], 0, 0)
    def it(s, _):
        @pl.when(s == 1)
        def _():
            pt[...] = mm(o_ref[...], g_ref[...])
        a[...] = mm(pt[...], pt[...], 1, 1)
        for kb in range(3):
            k0 = kb*128
            D = [a[k0+8*g:k0+8*g+8, k0:k0+128] for g in range(16)]
            Li = chol_inv(D)
            for g in range(16):
                li[8*g:8*g+8, :] = Li[g]
            Q = mm(li[...], pt[k0:k0+128, :])
            o_ref[k0:k0+128, :] = Q
            if kb < 2:
                R = mm(li[...], a[k0:k0+128, k0+128:])
                a[k0+128:, k0+128:] -= mm(R, R, 0, 0)
                pt[k0+128:, :] -= mm(R, Q, 0, 0)
        return 0
    lax.fori_loop(0, 2, it, 0)

def qr(G, B, **kw):
    return pl.pallas_call(qr_kernel, out_shape=jax.ShapeDtypeStruct((384, 512), jnp.float32),
        in_specs=[pl.BlockSpec(memory_space=pltpu.VMEM)]*2, out_specs=pl.BlockSpec(memory_space=pltpu.VMEM),
        scratch_shapes=[pltpu.VMEM((384,512),jnp.float32), pltpu.VMEM((384,384),jnp.float32), pltpu.VMEM((128,128),jnp.float32)], name="qr", **kw)(G, B)


def body(tensor, start_basis):
    local_gram = lax.dot_general(
        tensor,
        tensor,
        (((0, 2), (0, 2)), ((), ())),
        precision=lax.Precision.HIGHEST,
        preferred_element_type=jnp.float32,
    )
    gram = lax.psum(local_gram, ("gx", "gy"))
    basis_t = qr(gram, start_basis)
    core_local = jnp.einsum(
        "ra,kac->krc",
        basis_t,
        tensor,
        precision=lax.Precision.HIGHEST,
        preferred_element_type=jnp.float32,
    )
    return lax.all_to_all(core_local, "gy", split_axis=1, concat_axis=2, tiled=True)


def solution(mesh):
    placed = (P("gx", None, "gy"), P())
    return jax.shard_map(
        body, mesh=mesh, in_specs=placed, out_specs=P("gx", "gy", None), check_vma=False
    )
```

```python
import jax
import jax.numpy as jnp
from jax import lax
from jax.experimental import pallas as pl
from jax.experimental.pallas import tpu as pltpu
from jax.sharding import PartitionSpec as P
MESH = pl.DeviceIdType.MESH
BF = jnp.bfloat16
BLOCKS = [(i, j) for i in range(4) for j in range(i + 1)]
OFFS = sorted(((dx, dy) for dx in range(4) for dy in range(4)), key=lambda o: -(min(o[0], 4 - o[0]) + min(o[1], 4 - o[1])))
SELF = 15
NT = (((1,), (1,)), ((), ()))


def ar_kernel(t_ref, o_ref, tbuf, hb, lb, gp, ra, aa, rb, ab, rc, ac, tsem, sa, qa, sb, qb, sc, qc, sd, qd, se, qe):
    gx = lax.axis_index("gx")
    gy = lax.axis_index("gy")
    x, y, z, c = gx // 4, gx % 4, gy // 2, gy % 2
    mate = z * 2 + 1 - c

    def plane(k, sign):
        dx, dy = OFFS[k]
        return ((x + sign * dx + 4) % 4) * 4 + (y + sign * dy + 4) % 4

    loads = [pltpu.make_async_copy(t_ref.at[pl.ds(4 * i, 4)], tbuf.at[pl.ds(4 * i, 4)], tsem.at[i]) for i in range(4)]
    for cp in loads:
        cp.start()
    barrier = pltpu.get_barrier_semaphore()
    pl.semaphore_signal(barrier, inc=1, device_id=(gx, mate), device_id_type=MESH)
    for k in range(15):
        pl.semaphore_signal(barrier, inc=1, device_id=(plane(k, 1), gy), device_id_type=MESH)
    for d in range(1, 4):
        pl.semaphore_signal(barrier, inc=1, device_id=(gx, ((z + d) % 4) * 2 + c), device_id_type=MESH)

    for i in range(4):
        loads[i].wait()
        for s in range(4 * i, 4 * i + 4):
            v = tbuf[s]
            h = v.astype(BF)
            hb[:, 128 * s:128 * s + 128] = h
            lb[:, 128 * s:128 * s + 128] = (v - h.astype(jnp.float32)).astype(BF)

    def dot(a, b):
        return lax.dot_general(a, b, NT, preferred_element_type=jnp.float32)

    for (r0, c0) in ((0, 0), (256, 0), (256, 256)):
        hr, lr = hb[r0:r0 + 256, :], lb[r0:r0 + 256, :]
        hc, lc = hb[c0:c0 + 256, :], lb[c0:c0 + 256, :]
        g = dot(hr, hc) + dot(hr, lc) + dot(lr, hc)
        for n, (i, j) in enumerate(BLOCKS):
            if r0 <= 128 * i < r0 + 256 and c0 <= 128 * j < c0 + 256:
                gp[16 * n:16 * n + 16] = g[128 * i - r0:128 * i - r0 + 128, 128 * j - c0:128 * j - c0 + 128].reshape(16, 8, 128)

    pl.semaphore_wait(barrier, 19)
    pieces = lambda core, g: pl.ds(80 * core + 5 * g, 5)

    def remote(src, dst, ss, rs, dev):
        return pltpu.make_async_remote_copy(src_ref=src, dst_ref=dst, send_sem=ss, recv_sem=rs, device_id=dev, device_id_type=MESH)

    A = [remote(gp.at[pieces(1 - c, plane(k, 1))], ra.at[k], sa.at[k], qa.at[k], (gx, mate)) for k in range(16)]
    for cp in A:
        cp.start()
    B = []
    for k in range(16):
        A[k].wait_recv()
        aa[k] = gp[pieces(c, plane(k, 1))] + ra[k]
        if k != SELF:
            cp = remote(aa.at[k], rb.at[k], sb.at[k], qb.at[k], (plane(k, 1), gy))
            cp.start()
            B.append(cp)
    total = aa[SELF]
    for k in range(14, -1, -1):
        B[k].wait_recv()
        total = total + rb[k]
    ab[...] = total
    rc[z] = total
    C = []
    for d in range(1, 4):
        cp = remote(ab, rc.at[z], sc.at[d], qc.at[d], (gx, ((z + d) % 4) * 2 + c))
        cp.start()
        C.append(cp)
    for cp in C:
        cp.wait_recv()
    total = (rc[0] + rc[1]) + (rc[2] + rc[3])
    ac[...] = total
    mine = pieces(c, gx)
    D = []
    for k in range(15):
        cp = remote(ac, o_ref.at[mine], sd.at[k], qd.at[k], (plane(k, 1), gy))
        cp.start()
        D.append(cp)
    o_ref[mine] = total
    E = [remote(ac, o_ref.at[mine], se.at[SELF], qe.at[SELF], (gx, mate))]
    E[0].start()
    for k in range(14, -1, -1):
        D[k].wait_recv()
        spot = pieces(c, plane(k, -1))
        cp = remote(o_ref.at[spot], o_ref.at[spot], se.at[k], qe.at[k], (gx, mate))
        cp.start()
        E.append(cp)
    for cp in E:
        cp.wait_recv()
    for cp in A + B + C + D + E:
        cp.wait_send()


def gram_sum(tensor):
    f = jnp.float32
    V, D = pltpu.VMEM, pltpu.SemaphoreType.DMA
    return pl.pallas_call(
        ar_kernel,
        out_shape=jax.ShapeDtypeStruct((160, 8, 128), f),
        in_specs=[pl.BlockSpec(memory_space=pl.ANY)],
        out_specs=pl.BlockSpec(memory_space=pltpu.VMEM),
        scratch_shapes=[
            V((16, 512, 128), f), V((512, 2048), BF), V((512, 2048), BF),
            V((160, 8, 128), f), V((16, 5, 8, 128), f), V((16, 5, 8, 128), f), V((16, 5, 8, 128), f),
            V((5, 8, 128), f), V((4, 5, 8, 128), f), V((5, 8, 128), f),
            D((4,)), D((16,)), D((16,)), D((16,)), D((16,)), D((4,)), D((4,)), D((16,)), D((16,)), D((16,)), D((16,)),
        ],
        compiler_params=pltpu.CompilerParams(collective_id=0, has_side_effects=True, vmem_limit_bytes=40 << 20),
        name="gram_sum",
    )(tensor)


HI = lax.Precision.HIGHEST
def mm(a, b, ca=1, cb=0):
    return lax.dot_general(a, b, (((ca,), (cb,)), ((), ())), precision=HI, preferred_element_type=jnp.float32)

def rep(x):
    return jnp.broadcast_to(x, (8, 128))

def chol_inv(D):
    A = list(D)
    row = lax.broadcasted_iota(jnp.int32, (8, 128), 0)
    lane = lax.broadcasted_iota(jnp.int32, (8, 128), 1)
    Z = [jnp.where(lane == row + 8 * g, 1.0, 0.0).astype(jnp.float32) for g in range(16)]
    out = []
    for p in range(16):
        c = 8 * p
        S = [[rep(A[p][i:i+1, c+j:c+j+1]) for j in range(i+1)] for i in range(8)]
        V = [rep(A[p][i:i+1, :]) for i in range(8)]
        U = [rep(Z[p][i:i+1, :]) for i in range(8)]
        L = [[None]*8 for _ in range(8)]
        r = [None]*8
        for j in range(8):
            r[j] = lax.rsqrt(S[j][j])
            for i in range(j+1, 8):
                L[i][j] = S[i][j] * r[j]
            for i in range(j+1, 8):
                for k in range(j+1, i+1):
                    S[i][k] = S[i][k] - L[i][j] * L[k][j]
            V[j] = V[j] * r[j]
            U[j] = U[j] * r[j]
            for i in range(j+1, 8):
                V[i] = V[i] - L[i][j] * V[j]
                U[i] = U[i] - L[i][j] * U[j]
        o = U[0]
        for i in range(1, 8):
            o = jnp.where(row == i, U[i], o)
        out.append(o)
        if p == 15:
            break
        F = list(V); FU = list(U)
        for j in range(7, -1, -1):
            F[j] = F[j] * r[j]
            FU[j] = FU[j] * r[j]
            for i in range(j):
                F[i] = F[i] - L[j][i] * F[j]
                FU[i] = FU[i] - L[j][i] * FU[j]
        for g in range(p+1, 16):
            X = [jnp.broadcast_to(A[g][:, c+j:c+j+1], (8, 128)) for j in range(8)]
            def acc(Y, F):
                t = [X[j]*F[j] for j in range(8)]
                t = [t[0]+t[1], t[2]+t[3], t[4]+t[5], t[6]+t[7]]
                return Y - ((t[0]+t[1]) + (t[2]+t[3]))
            Z[g] = acc(Z[g], FU)
            A[g] = acc(A[g], F)
    return out

def qr_kernel(p_ref, b_ref, o_ref, g_ref, pt, a, li):
    n = 0
    for i in range(4):
        for j in range(i + 1):
            blk = p_ref[16*n:16*n+16].reshape(128, 128)
            g_ref[128*i:128*i+128, 128*j:128*j+128] = blk
            if j < i:
                g_ref[128*j:128*j+128, 128*i:128*i+128] = blk.T
            n += 1
    pt[...] = mm(b_ref[...], g_ref[...], 0, 0)
    def it(s, _):
        @pl.when(s == 1)
        def _():
            pt[...] = mm(o_ref[...], g_ref[...])
        a[...] = mm(pt[...], pt[...], 1, 1)
        for kb in range(3):
            k0 = kb*128
            D = [a[k0+8*g:k0+8*g+8, k0:k0+128] for g in range(16)]
            Li = chol_inv(D)
            for g in range(16):
                li[8*g:8*g+8, :] = Li[g]
            Q = mm(li[...], pt[k0:k0+128, :])
            o_ref[k0:k0+128, :] = Q
            if kb < 2:
                R = mm(li[...], a[k0:k0+128, k0+128:])
                a[k0+128:, k0+128:] -= mm(R, R, 0, 0)
                pt[k0+128:, :] -= mm(R, Q, 0, 0)
        return 0
    lax.fori_loop(0, 2, it, 0)

def qr(G, B, **kw):
    return pl.pallas_call(qr_kernel, out_shape=jax.ShapeDtypeStruct((384, 512), jnp.float32),
        in_specs=[pl.BlockSpec(memory_space=pltpu.VMEM)]*2, out_specs=pl.BlockSpec(memory_space=pltpu.VMEM),
        scratch_shapes=[pltpu.VMEM((512,512),jnp.float32), pltpu.VMEM((384,512),jnp.float32), pltpu.VMEM((384,384),jnp.float32), pltpu.VMEM((128,128),jnp.float32)], name="qr", **kw)(G, B)


def body(tensor, start_basis):
    basis_t = qr(gram_sum(tensor), start_basis)
    core_local = jnp.einsum(
        "ra,kac->krc",
        basis_t,
        tensor,
        precision=lax.Precision.HIGHEST,
        preferred_element_type=jnp.float32,
    )
    return lax.all_to_all(core_local, "gy", split_axis=1, concat_axis=2, tiled=True)


def solution(mesh):
    placed = (P("gx", None, "gy"), P())
    return jax.shard_map(
        body, mesh=mesh, in_specs=placed, out_specs=P("gx", "gy", None), check_vma=False
    )
```

```python
import jax
import jax.numpy as jnp
from jax import lax
from jax.experimental import pallas as pl
from jax.experimental.pallas import tpu as pltpu
from jax.sharding import PartitionSpec as P
MESH = pl.DeviceIdType.MESH
BF = jnp.bfloat16
BLOCKS = [(i, j) for i in range(4) for j in range(i + 1)]
OFFS = sorted(((dx, dy) for dx in range(4) for dy in range(4)), key=lambda o: -(min(o[0], 4 - o[0]) + min(o[1], 4 - o[1])))
SELF = 15
NT = (((1,), (1,)), ((), ()))


def ar_kernel(t_ref, o_ref, tbuf, hb, lb, gp, ra, aa, rb, ab, rc, ac, tsem, sa, qa, sb, qb, sc, qc, sd, qd, se, qe):
    gx = lax.axis_index("gx")
    gy = lax.axis_index("gy")
    x, y, z, c = gx // 4, gx % 4, gy // 2, gy % 2
    mate = z * 2 + 1 - c

    def plane(k, sign):
        dx, dy = OFFS[k]
        return ((x + sign * dx + 4) % 4) * 4 + (y + sign * dy + 4) % 4

    loads = [pltpu.make_async_copy(t_ref.at[pl.ds(4 * i, 4)], tbuf.at[pl.ds(4 * i, 4)], tsem.at[i]) for i in range(4)]
    for cp in loads:
        cp.start()
    barrier = pltpu.get_barrier_semaphore()
    pl.semaphore_signal(barrier, inc=1, device_id=(gx, mate), device_id_type=MESH)
    for k in range(15):
        pl.semaphore_signal(barrier, inc=1, device_id=(plane(k, 1), gy), device_id_type=MESH)
    for d in range(1, 4):
        pl.semaphore_signal(barrier, inc=1, device_id=(gx, ((z + d) % 4) * 2 + c), device_id_type=MESH)

    for i in range(4):
        loads[i].wait()
        for s in range(4 * i, 4 * i + 4):
            v = tbuf[s]
            h = v.astype(BF)
            hb[:, 128 * s:128 * s + 128] = h
            lb[:, 128 * s:128 * s + 128] = (v - h.astype(jnp.float32)).astype(BF)

    def dot(a, b):
        return lax.dot_general(a, b, NT, preferred_element_type=jnp.float32)

    for (r0, c0) in ((0, 0), (256, 0), (256, 256)):
        hr, lr = hb[r0:r0 + 256, :], lb[r0:r0 + 256, :]
        hc, lc = hb[c0:c0 + 256, :], lb[c0:c0 + 256, :]
        g = dot(hr, hc) + dot(hr, lc) + dot(lr, hc)
        for n, (i, j) in enumerate(BLOCKS):
            if r0 <= 128 * i < r0 + 256 and c0 <= 128 * j < c0 + 256:
                gp[16 * n:16 * n + 16] = g[128 * i - r0:128 * i - r0 + 128, 128 * j - c0:128 * j - c0 + 128].reshape(16, 8, 128)

    pl.semaphore_wait(barrier, 19)
    pieces = lambda core, g: pl.ds(80 * core + 5 * g, 5)

    def remote(src, dst, ss, rs, dev):
        return pltpu.make_async_remote_copy(src_ref=src, dst_ref=dst, send_sem=ss, recv_sem=rs, device_id=dev, device_id_type=MESH)

    A = [remote(gp.at[pieces(1 - c, plane(k, 1))], ra.at[k], sa.at[k], qa.at[k], (gx, mate)) for k in range(16)]
    for cp in A:
        cp.start()
    B = []
    for k in range(16):
        A[k].wait_recv()
        aa[k] = gp[pieces(c, plane(k, 1))] + ra[k]
        if k != SELF:
            cp = remote(aa.at[k], rb.at[k], sb.at[k], qb.at[k], (plane(k, 1), gy))
            cp.start()
            B.append(cp)
    total = aa[SELF]
    for k in range(14, -1, -1):
        B[k].wait_recv()
        total = total + rb[k]
    ab[...] = total
    rc[z] = total
    C = []
    for d in range(1, 4):
        cp = remote(ab, rc.at[z], sc.at[d], qc.at[d], (gx, ((z + d) % 4) * 2 + c))
        cp.start()
        C.append(cp)
    for cp in C:
        cp.wait_recv()
    total = (rc[0] + rc[1]) + (rc[2] + rc[3])
    ac[...] = total
    mine = pieces(c, gx)
    D = []
    for k in range(15):
        cp = remote(ac, o_ref.at[mine], sd.at[k], qd.at[k], (plane(k, 1), gy))
        cp.start()
        D.append(cp)
    o_ref[mine] = total
    E = [remote(ac, o_ref.at[mine], se.at[SELF], qe.at[SELF], (gx, mate))]
    E[0].start()
    for k in range(14, -1, -1):
        D[k].wait_recv()
        spot = pieces(c, plane(k, -1))
        cp = remote(o_ref.at[spot], o_ref.at[spot], se.at[k], qe.at[k], (gx, mate))
        cp.start()
        E.append(cp)
    for cp in E:
        cp.wait_recv()
    for cp in A + B + C + D + E:
        cp.wait_send()


def gram_sum(tensor):
    f = jnp.float32
    V, D = pltpu.VMEM, pltpu.SemaphoreType.DMA
    return pl.pallas_call(
        ar_kernel,
        out_shape=jax.ShapeDtypeStruct((160, 8, 128), f),
        in_specs=[pl.BlockSpec(memory_space=pl.ANY)],
        out_specs=pl.BlockSpec(memory_space=pltpu.VMEM),
        scratch_shapes=[
            V((16, 512, 128), f), V((512, 2048), BF), V((512, 2048), BF),
            V((160, 8, 128), f), V((16, 5, 8, 128), f), V((16, 5, 8, 128), f), V((16, 5, 8, 128), f),
            V((5, 8, 128), f), V((4, 5, 8, 128), f), V((5, 8, 128), f),
            D((4,)), D((16,)), D((16,)), D((16,)), D((16,)), D((4,)), D((4,)), D((16,)), D((16,)), D((16,)), D((16,)),
        ],
        compiler_params=pltpu.CompilerParams(collective_id=0, has_side_effects=True, vmem_limit_bytes=62 << 20),
        name="gram_sum",
    )(tensor)


HI = lax.Precision.HIGHEST
def mm(a, b, ca=1, cb=0):
    return lax.dot_general(a, b, (((ca,), (cb,)), ((), ())), precision=HI, preferred_element_type=jnp.float32)

def rep(x):
    return jnp.broadcast_to(x, (8, 128))

def chol_inv(D):
    A = list(D)
    row = lax.broadcasted_iota(jnp.int32, (8, 128), 0)
    lane = lax.broadcasted_iota(jnp.int32, (8, 128), 1)
    Z = [jnp.where(lane == row + 8 * g, 1.0, 0.0).astype(jnp.float32) for g in range(16)]
    out = []
    for p in range(16):
        c = 8 * p
        S = [[rep(A[p][i:i+1, c+j:c+j+1]) for j in range(i+1)] for i in range(8)]
        V = [rep(A[p][i:i+1, :]) for i in range(8)]
        U = [rep(Z[p][i:i+1, :]) for i in range(8)]
        L = [[None]*8 for _ in range(8)]
        r = [None]*8
        for j in range(8):
            r[j] = lax.rsqrt(S[j][j])
            for i in range(j+1, 8):
                L[i][j] = S[i][j] * r[j]
            for i in range(j+1, 8):
                for k in range(j+1, i+1):
                    S[i][k] = S[i][k] - L[i][j] * L[k][j]
            V[j] = V[j] * r[j]
            U[j] = U[j] * r[j]
            for i in range(j+1, 8):
                V[i] = V[i] - L[i][j] * V[j]
                U[i] = U[i] - L[i][j] * U[j]
        o = U[0]
        for i in range(1, 8):
            o = jnp.where(row == i, U[i], o)
        out.append(o)
        if p == 15:
            break
        F = list(V); FU = list(U)
        for j in range(7, -1, -1):
            F[j] = F[j] * r[j]
            FU[j] = FU[j] * r[j]
            for i in range(j):
                F[i] = F[i] - L[j][i] * F[j]
                FU[i] = FU[i] - L[j][i] * FU[j]
        for g in range(p+1, 16):
            X = [jnp.broadcast_to(A[g][:, c+j:c+j+1], (8, 128)) for j in range(8)]
            def acc(Y, F):
                t = [X[j]*F[j] for j in range(8)]
                t = [t[0]+t[1], t[2]+t[3], t[4]+t[5], t[6]+t[7]]
                return Y - ((t[0]+t[1]) + (t[2]+t[3]))
            Z[g] = acc(Z[g], FU)
            A[g] = acc(A[g], F)
    return out

def qr_kernel(p_ref, b_ref, o_ref, g_ref, pt, a, li):
    n = 0
    for i in range(4):
        for j in range(i + 1):
            blk = p_ref[16*n:16*n+16].reshape(128, 128)
            g_ref[128*i:128*i+128, 128*j:128*j+128] = blk
            if j < i:
                g_ref[128*j:128*j+128, 128*i:128*i+128] = blk.T
            n += 1
    pt[...] = mm(b_ref[...], g_ref[...], 0, 0)
    def it(s, _):
        @pl.when(s == 1)
        def _():
            pt[...] = mm(o_ref[...], g_ref[...])
        a[...] = mm(pt[...], pt[...], 1, 1)
        for kb in range(3):
            k0 = kb*128
            D = [a[k0+8*g:k0+8*g+8, k0:k0+128] for g in range(16)]
            Li = chol_inv(D)
            for g in range(16):
                li[8*g:8*g+8, :] = Li[g]
            Q = mm(li[...], pt[k0:k0+128, :])
            o_ref[k0:k0+128, :] = Q
            if kb < 2:
                R = mm(li[...], a[k0:k0+128, k0+128:])
                a[k0+128:, k0+128:] -= mm(R, R, 0, 0)
                pt[k0+128:, :] -= mm(R, Q, 0, 0)
        return 0
    lax.fori_loop(0, 2, it, 0)

def qr(G, B, **kw):
    return pl.pallas_call(qr_kernel, out_shape=jax.ShapeDtypeStruct((384, 512), jnp.float32),
        in_specs=[pl.BlockSpec(memory_space=pltpu.VMEM)]*2, out_specs=pl.BlockSpec(memory_space=pltpu.VMEM),
        scratch_shapes=[pltpu.VMEM((512,512),jnp.float32), pltpu.VMEM((384,512),jnp.float32), pltpu.VMEM((384,384),jnp.float32), pltpu.VMEM((128,128),jnp.float32)], name="qr", **kw)(G, B)


RELS = [(2, 0), (2, 1), (1, 0), (3, 0), (1, 1), (3, 1), (0, 1)]
GROUPS = [(0, 2), (2, 4), (4, 8), (8, 12), (12, 16)]


def core_kernel(q_ref, t_ref, o_ref, tbuf, qh, ql, y, tsem, ssem, rsem, osem):
    gx = lax.axis_index("gx")
    gy = lax.axis_index("gy")
    z, c = gy // 2, gy % 2

    def other(r):
        dz, dc = RELS[r]
        return ((z + dz) % 4) * 2 + (c + dc) % 2

    loads = [pltpu.make_async_copy(t_ref.at[pl.ds(a, b - a)], tbuf.at[pl.ds(a, b - a)], tsem.at[n]) for n, (a, b) in enumerate(GROUPS)]
    for cp in loads:
        cp.start()
    barrier = pltpu.get_barrier_semaphore()
    for r in range(7):
        pl.semaphore_signal(barrier, inc=1, device_id=(gx, other(r)), device_id_type=pl.DeviceIdType.MESH)
    v = q_ref[...]
    h = v.astype(jnp.bfloat16)
    qh[...] = h
    ql[...] = (v - h.astype(jnp.float32)).astype(jnp.bfloat16)

    def dot(a, b):
        return jnp.dot(a, b, preferred_element_type=jnp.float32)

    spot = pl.ds(pl.multiple_of(gy * 128, 128), 128)
    sends = []
    for n, (a, b) in enumerate(GROUPS):
        loads[n].wait()
        for k in range(a, b, 2):
            v = jnp.concatenate([tbuf[k], tbuf[k + 1]], axis=1)
            th = v.astype(jnp.bfloat16)
            tl = (v - th.astype(jnp.float32)).astype(jnp.bfloat16)
            out = dot(qh[...], th) + dot(qh[...], tl) + dot(ql[...], th)
            y[k] = out[:, :128]
            y[k + 1] = out[:, 128:]
        if n == 0:
            pl.semaphore_wait(barrier, 7)
        for r in range(7):
            cp = pltpu.make_async_remote_copy(
                src_ref=y.at[pl.ds(a, b - a), pl.ds(pl.multiple_of(48 * other(r), 8), 48)],
                dst_ref=o_ref.at[pl.ds(a, b - a), pl.ds(0, 48), spot],
                send_sem=ssem.at[r, n], recv_sem=rsem.at[r, n],
                device_id=(gx, other(r)), device_id_type=pl.DeviceIdType.MESH)
            cp.start()
            sends.append(cp)
    own = pltpu.make_async_copy(y.at[pl.ds(0, 16), pl.ds(pl.multiple_of(48 * gy, 8), 48)], o_ref.at[pl.ds(0, 16), pl.ds(0, 48), spot], osem)
    own.start()
    for cp in sends:
        cp.wait()
    own.wait()


def core_out(basis_t, tensor):
    f = jnp.float32
    V, D = pltpu.VMEM, pltpu.SemaphoreType.DMA
    ng = len(GROUPS)
    return pl.pallas_call(
        core_kernel,
        out_shape=jax.ShapeDtypeStruct((16, 48, 1024), f),
        in_specs=[pl.BlockSpec(memory_space=pltpu.VMEM), pl.BlockSpec(memory_space=pl.ANY)],
        out_specs=pl.BlockSpec(memory_space=pl.ANY),
        scratch_shapes=[V((16, 512, 128), f), V((384, 512), jnp.bfloat16), V((384, 512), jnp.bfloat16), V((16, 384, 128), f),
                        D((ng,)), D((7, ng)), D((7, ng)), D],
        compiler_params=pltpu.CompilerParams(collective_id=1, has_side_effects=True, vmem_limit_bytes=62 << 20),
        name="core_out",
    )(basis_t, tensor)


def body(tensor, start_basis):
    basis_t = qr(gram_sum(tensor), start_basis)
    return core_out(basis_t, tensor)


def solution(mesh):
    placed = (P("gx", None, "gy"), P())
    return jax.shard_map(
        body, mesh=mesh, in_specs=placed, out_specs=P("gx", "gy", None), check_vma=False
    )
```

```python
import jax
import jax.numpy as jnp
from jax import lax
from jax.experimental import pallas as pl
from jax.experimental.pallas import tpu as pltpu
from jax.sharding import PartitionSpec as P
MESH = pl.DeviceIdType.MESH
BF = jnp.bfloat16
BLOCKS = [(i, j) for i in range(4) for j in range(i + 1)]
OFFS = sorted(((dx, dy) for dx in range(4) for dy in range(4)), key=lambda o: -(min(o[0], 4 - o[0]) + min(o[1], 4 - o[1])))
SELF = 15
NT = (((1,), (1,)), ((), ()))


def ar_kernel(t_ref, o_ref, tbuf, hb, lb, gp, ra, aa, rb, ab, rc, ac, tsem, sa, qa, sb, qb, sc, qc, sd, qd, se, qe):
    gx = lax.axis_index("gx")
    gy = lax.axis_index("gy")
    x, y, z, c = gx // 4, gx % 4, gy // 2, gy % 2
    mate = z * 2 + 1 - c

    def plane(k, sign):
        dx, dy = OFFS[k]
        return ((x + sign * dx + 4) % 4) * 4 + (y + sign * dy + 4) % 4

    loads = [pltpu.make_async_copy(t_ref.at[pl.ds(4 * i, 4)], tbuf.at[pl.ds(4 * i, 4)], tsem.at[i]) for i in range(4)]
    for cp in loads:
        cp.start()
    barrier = pltpu.get_barrier_semaphore()
    pl.semaphore_signal(barrier, inc=1, device_id=(gx, mate), device_id_type=MESH)
    for k in range(15):
        pl.semaphore_signal(barrier, inc=1, device_id=(plane(k, 1), gy), device_id_type=MESH)
    for d in range(1, 4):
        pl.semaphore_signal(barrier, inc=1, device_id=(gx, ((z + d) % 4) * 2 + c), device_id_type=MESH)

    for i in range(4):
        loads[i].wait()
        for s in range(4 * i, 4 * i + 4):
            v = tbuf[s]
            h = v.astype(BF)
            hb[:, 128 * s:128 * s + 128] = h
            lb[:, 128 * s:128 * s + 128] = (v - h.astype(jnp.float32)).astype(BF)

    def dot(a, b):
        return lax.dot_general(a, b, NT, preferred_element_type=jnp.float32)

    for (r0, c0) in ((0, 0), (256, 0), (256, 256)):
        hr, lr = hb[r0:r0 + 256, :], lb[r0:r0 + 256, :]
        hc, lc = hb[c0:c0 + 256, :], lb[c0:c0 + 256, :]
        g = dot(hr, hc) + dot(hr, lc) + dot(lr, hc)
        for n, (i, j) in enumerate(BLOCKS):
            if r0 <= 128 * i < r0 + 256 and c0 <= 128 * j < c0 + 256:
                gp[16 * n:16 * n + 16] = g[128 * i - r0:128 * i - r0 + 128, 128 * j - c0:128 * j - c0 + 128].reshape(16, 8, 128)

    pl.semaphore_wait(barrier, 19)
    pieces = lambda core, g: pl.ds(80 * core + 5 * g, 5)

    def remote(src, dst, ss, rs, dev):
        return pltpu.make_async_remote_copy(src_ref=src, dst_ref=dst, send_sem=ss, recv_sem=rs, device_id=dev, device_id_type=MESH)

    A = [remote(gp.at[pieces(1 - c, plane(k, 1))], ra.at[k], sa.at[k], qa.at[k], (gx, mate)) for k in range(16)]
    for cp in A:
        cp.start()
    B = []
    for k in range(16):
        A[k].wait_recv()
        aa[k] = gp[pieces(c, plane(k, 1))] + ra[k]
        if k != SELF:
            cp = remote(aa.at[k], rb.at[k], sb.at[k], qb.at[k], (plane(k, 1), gy))
            cp.start()
            B.append(cp)
    total = aa[SELF]
    for k in range(14, -1, -1):
        B[k].wait_recv()
        total = total + rb[k]
    ab[...] = total
    rc[z] = total
    C = []
    for d in range(1, 4):
        cp = remote(ab, rc.at[z], sc.at[d], qc.at[d], (gx, ((z + d) % 4) * 2 + c))
        cp.start()
        C.append(cp)
    for cp in C:
        cp.wait_recv()
    total = (rc[0] + rc[1]) + (rc[2] + rc[3])
    ac[...] = total
    mine = pieces(c, gx)
    D = []
    for k in range(15):
        cp = remote(ac, o_ref.at[mine], sd.at[k], qd.at[k], (plane(k, 1), gy))
        cp.start()
        D.append(cp)
    o_ref[mine] = total
    E = [remote(ac, o_ref.at[mine], se.at[SELF], qe.at[SELF], (gx, mate))]
    E[0].start()
    for k in range(14, -1, -1):
        D[k].wait_recv()
        spot = pieces(c, plane(k, -1))
        cp = remote(o_ref.at[spot], o_ref.at[spot], se.at[k], qe.at[k], (gx, mate))
        cp.start()
        E.append(cp)
    for cp in E:
        cp.wait_recv()
    for cp in A + B + C + D + E:
        cp.wait_send()


def gram_sum(tensor):
    f = jnp.float32
    V, D = pltpu.VMEM, pltpu.SemaphoreType.DMA
    return pl.pallas_call(
        ar_kernel,
        out_shape=jax.ShapeDtypeStruct((160, 8, 128), f),
        in_specs=[pl.BlockSpec(memory_space=pl.ANY)],
        out_specs=pl.BlockSpec(memory_space=pltpu.VMEM),
        scratch_shapes=[
            V((16, 512, 128), f), V((512, 2048), BF), V((512, 2048), BF),
            V((160, 8, 128), f), V((16, 5, 8, 128), f), V((16, 5, 8, 128), f), V((16, 5, 8, 128), f),
            V((5, 8, 128), f), V((4, 5, 8, 128), f), V((5, 8, 128), f),
            D((4,)), D((16,)), D((16,)), D((16,)), D((16,)), D((4,)), D((4,)), D((16,)), D((16,)), D((16,)), D((16,)),
        ],
        compiler_params=pltpu.CompilerParams(collective_id=0, has_side_effects=True, vmem_limit_bytes=62 << 20),
        name="gram_sum",
    )(tensor)


HI = lax.Precision.HIGHEST
def mm(a, b, ca=1, cb=0):
    return lax.dot_general(a, b, (((ca,), (cb,)), ((), ())), precision=HI, preferred_element_type=jnp.float32)

def rep(x):
    return jnp.broadcast_to(x, (8, 128))

def chol_inv(D):
    A = list(D)
    row = lax.broadcasted_iota(jnp.int32, (8, 128), 0)
    lane = lax.broadcasted_iota(jnp.int32, (8, 128), 1)
    Z = [jnp.where(lane == row + 8 * g, 1.0, 0.0).astype(jnp.float32) for g in range(16)]
    out = []
    for p in range(16):
        c = 8 * p
        S = [[rep(A[p][i:i+1, c+j:c+j+1]) for j in range(i+1)] for i in range(8)]
        V = [rep(A[p][i:i+1, :]) for i in range(8)]
        U = [rep(Z[p][i:i+1, :]) for i in range(8)]
        L = [[None]*8 for _ in range(8)]
        r = [None]*8
        for j in range(8):
            r[j] = lax.rsqrt(S[j][j])
            for i in range(j+1, 8):
                L[i][j] = S[i][j] * r[j]
            for i in range(j+1, 8):
                for k in range(j+1, i+1):
                    S[i][k] = S[i][k] - L[i][j] * L[k][j]
            V[j] = V[j] * r[j]
            U[j] = U[j] * r[j]
            for i in range(j+1, 8):
                V[i] = V[i] - L[i][j] * V[j]
                U[i] = U[i] - L[i][j] * U[j]
        o = U[0]
        for i in range(1, 8):
            o = jnp.where(row == i, U[i], o)
        out.append(o)
        if p == 15:
            break
        F = list(V); FU = list(U)
        for j in range(7, -1, -1):
            F[j] = F[j] * r[j]
            FU[j] = FU[j] * r[j]
            for i in range(j):
                F[i] = F[i] - L[j][i] * F[j]
                FU[i] = FU[i] - L[j][i] * FU[j]
        for g in range(p+1, 16):
            X = [jnp.broadcast_to(A[g][:, c+j:c+j+1], (8, 128)) for j in range(8)]
            def acc(Y, F):
                t = [X[j]*F[j] for j in range(8)]
                t = [t[0]+t[1], t[2]+t[3], t[4]+t[5], t[6]+t[7]]
                return Y - ((t[0]+t[1]) + (t[2]+t[3]))
            Z[g] = acc(Z[g], FU)
            A[g] = acc(A[g], F)
    return out

def sweep(pt, a, o_ref, li):
    a[...] = mm(pt[...], pt[...], 1, 1)

    def block(kb, _):
        k0 = pl.multiple_of(kb * 128, 128)
        Li = chol_inv([a[pl.ds(k0 + 8 * g, 8), pl.ds(k0, 128)] for g in range(16)])
        for g in range(16):
            li[8 * g:8 * g + 8, :] = Li[g]
        for n in range(3):
            @pl.when(kb == n)
            def _():
                lo, hi = 128 * n, 128 * n + 128
                Q = mm(li[...], pt[lo:hi, :])
                o_ref[lo:hi, :] = Q
                if n < 2:
                    R = mm(li[...], a[lo:hi, hi:])
                    a[hi:, hi:] -= mm(R, R, 0, 0)
                    pt[hi:, :] -= mm(R, Q, 0, 0)
        return 0

    lax.fori_loop(0, 3, block, 0)


def first_kernel(p_ref, b_ref, g_ref, o_ref, pt, a, li):
    n = 0
    for i in range(4):
        for j in range(i + 1):
            blk = p_ref[16 * n:16 * n + 16].reshape(128, 128)
            g_ref[128 * i:128 * i + 128, 128 * j:128 * j + 128] = blk
            if j < i:
                g_ref[128 * j:128 * j + 128, 128 * i:128 * i + 128] = blk.T
            n += 1
    pt[...] = mm(b_ref[...], g_ref[...], 0, 0)
    sweep(pt, a, o_ref, li)


def second_kernel(g_ref, q_ref, o_ref, pt, a, li):
    pt[...] = mm(q_ref[...], g_ref[...])
    sweep(pt, a, o_ref, li)


SCRATCH = [pltpu.VMEM((384, 512), jnp.float32), pltpu.VMEM((384, 384), jnp.float32), pltpu.VMEM((128, 128), jnp.float32)]
WHOLE = pl.BlockSpec(memory_space=pltpu.VMEM)
COST = pl.CostEstimate(flops=2000000000, bytes_accessed=3000000, transcendentals=0)


def sweep_first(packed, start):
    return pl.pallas_call(
        first_kernel,
        out_shape=(jax.ShapeDtypeStruct((512, 512), jnp.float32), jax.ShapeDtypeStruct((384, 512), jnp.float32)),
        in_specs=[WHOLE] * 2, out_specs=(WHOLE, WHOLE), scratch_shapes=SCRATCH, cost_estimate=COST, name="sweep_first",
    )(packed, start)


def sweep_second(gram, basis_t):
    return pl.pallas_call(
        second_kernel,
        out_shape=jax.ShapeDtypeStruct((384, 512), jnp.float32),
        in_specs=[WHOLE] * 2, out_specs=WHOLE, scratch_shapes=SCRATCH, cost_estimate=COST, name="sweep_second",
    )(gram, basis_t)


RELS = [(2, 0), (2, 1), (1, 0), (3, 0), (1, 1), (3, 1), (0, 1)]
KG = 8
GROUPS = [(0, 2), (2, 4), (4, 8)]


def core_kernel(q_ref, t_ref, g1a, g1b, g3a, g3b, g2a, g2b, o_ref, tbuf, gbuf, qh, ql, y, yg, tsem, gsem, ssem, rsem, xsem, wsem, osem):
    gx = lax.axis_index("gx")
    gy = lax.axis_index("gy")
    z, c = gy // 2, gy % 2

    def other(r):
        dz, dc = RELS[r]
        return ((z + dz) % 4) * 2 + (c + dc) % 2

    na = 16 - KG
    loads = [pltpu.make_async_copy(t_ref.at[pl.ds(KG + a, b - a)], tbuf.at[pl.ds(a, b - a)], tsem.at[n]) for n, (a, b) in enumerate(GROUPS)]
    half = KG // 2
    gloads = [[pltpu.make_async_copy(t_ref.at[pl.ds(half * n, half)] if r is None else r, gbuf.at[s, pl.ds(half * n, half)], gsem.at[s, n]) for n, r in enumerate(p)]
              for s, p in enumerate(((None, None), (g1a, g1b), (g3a, g3b), (g2a, g2b)))]
    for cp in loads:
        cp.start()
    for cps in gloads:
        for cp in cps:
            cp.start()
    barrier = pltpu.get_barrier_semaphore()
    for r in range(7):
        pl.semaphore_signal(barrier, inc=1, device_id=(gx, other(r)), device_id_type=pl.DeviceIdType.MESH)
    v = q_ref[...]
    h = v.astype(jnp.bfloat16)
    qh[...] = h
    ql[...] = (v - h.astype(jnp.float32)).astype(jnp.bfloat16)

    def dot(a, b):
        return jnp.dot(a, b, preferred_element_type=jnp.float32)

    def split(v):
        th = v.astype(jnp.bfloat16)
        return th, (v - th.astype(jnp.float32)).astype(jnp.bfloat16)

    def cols(dev):
        return pl.ds(pl.multiple_of(dev * 128, 128), 128)

    sends = []
    for n, (a, b) in enumerate(GROUPS):
        loads[n].wait()
        for k in range(a, b, 2):
            th, tl = split(jnp.concatenate([tbuf[k], tbuf[k + 1]], axis=1))
            out = dot(qh[...], th) + dot(qh[...], tl) + dot(ql[...], th)
            y[k] = out[:, :128]
            y[k + 1] = out[:, 128:]
        if n == 0:
            pl.semaphore_wait(barrier, 7)
        for r in range(7):
            cp = pltpu.make_async_remote_copy(
                src_ref=y.at[pl.ds(a, b - a), pl.ds(pl.multiple_of(48 * other(r), 8), 48)],
                dst_ref=o_ref.at[pl.ds(KG + a, b - a), pl.ds(0, 48), cols(gy)],
                send_sem=ssem.at[r, n], recv_sem=rsem.at[r, n],
                device_id=(gx, other(r)), device_id_type=pl.DeviceIdType.MESH)
            cp.start()
            sends.append(cp)
    own = pltpu.make_async_copy(y.at[pl.ds(0, na), pl.ds(pl.multiple_of(48 * gy, 8), 48)], o_ref.at[pl.ds(KG, na), pl.ds(0, 48), cols(gy)], osem.at[4])
    own.start()
    rows = pl.ds(pl.multiple_of(96 * z, 32), 96)
    q2 = jnp.concatenate([qh[rows, :], ql[rows, :]], axis=0)
    locs = [own]
    for s, dz in enumerate((0, 3, 1, 2)):
        for cp in gloads[s]:
            cp.wait()
        for k in range(0, KG, 2):
            th, tl = split(jnp.concatenate([gbuf[s, k], gbuf[s, k + 1]], axis=1))
            o2 = dot(q2, th)
            out = o2[:96] + o2[96:] + dot(q2[:96], tl)
            for d in range(2):
                yg[s, 0, k + d] = out[:48, 128 * d:128 * d + 128]
                yg[s, 1, k + d] = out[48:, 128 * d:128 * d + 128]
        src = ((z + dz) % 4) * 2 + c
        cp = pltpu.make_async_remote_copy(
            src_ref=yg.at[s, 1 - c], dst_ref=o_ref.at[pl.ds(0, KG), pl.ds(0, 48), cols(src)],
            send_sem=xsem.at[s], recv_sem=wsem.at[s],
            device_id=(gx, z * 2 + 1 - c), device_id_type=pl.DeviceIdType.MESH)
        cp.start()
        sends.append(cp)
        cp = pltpu.make_async_copy(yg.at[s, c], o_ref.at[pl.ds(0, KG), pl.ds(0, 48), cols(src)], osem.at[s])
        cp.start()
        locs.append(cp)
    for cp in sends:
        cp.wait()
    for cp in locs:
        cp.wait()


def core_out(basis_t, tensor, below, above, far):
    f = jnp.float32
    V, D = pltpu.VMEM, pltpu.SemaphoreType.DMA
    ng = len(GROUPS)
    ANY = pl.BlockSpec(memory_space=pl.ANY)
    return pl.pallas_call(
        core_kernel,
        out_shape=jax.ShapeDtypeStruct((16, 48, 1024), f),
        in_specs=[pl.BlockSpec(memory_space=pltpu.VMEM)] + [ANY] * 7,
        out_specs=ANY,
        scratch_shapes=[V((16 - KG, 512, 128), f), V((4, KG, 512, 128), f), V((384, 512), jnp.bfloat16), V((384, 512), jnp.bfloat16),
                        V((16 - KG, 384, 128), f), V((4, 2, KG, 48, 128), f),
                        D((ng,)), D((4, 2)), D((7, ng)), D((7, ng)), D((4,)), D((4,)), D((5,))],
        compiler_params=pltpu.CompilerParams(collective_id=1, has_side_effects=True, vmem_limit_bytes=62 << 20),
        name="core_out",
    )(basis_t, tensor, *below, *above, *far)


def shift(x, d):
    pairs = [(zz * 2 + cc, ((zz + d) % 4) * 2 + cc) for zz in range(4) for cc in range(2)]
    return lax.ppermute(x, "gy", pairs)


def body(tensor, start_basis):
    half = KG // 2
    parts = (tensor[:half], tensor[half:KG])
    below = [shift(p, 1) for p in parts]
    above = [shift(p, -1) for p in parts]
    packed = gram_sum(tensor)
    gram, basis_t = sweep_first(packed, start_basis)
    gram, basis_t, below, above = lax.optimization_barrier((gram, basis_t, below, above))
    far = (shift(below[0], 1), shift(above[1], -1))
    basis_t = sweep_second(gram, basis_t)
    return core_out(basis_t, tensor, below, above, far)


def solution(mesh):
    placed = (P("gx", None, "gy"), P())
    return jax.shard_map(
        body, mesh=mesh, in_specs=placed, out_specs=P("gx", "gy", None), check_vma=False
    )
```

```python
import jax
import jax.numpy as jnp
from jax import lax
from jax.experimental import pallas as pl
from jax.experimental.pallas import tpu as pltpu
from jax.sharding import PartitionSpec as P
MESH = pl.DeviceIdType.MESH
BF = jnp.bfloat16
BLOCKS = [(i, j) for i in range(4) for j in range(i + 1)]
OFFS = sorted(((dx, dy) for dx in range(4) for dy in range(4)), key=lambda o: -(min(o[0], 4 - o[0]) + min(o[1], 4 - o[1])))
SELF = 15
NT = (((1,), (1,)), ((), ()))


def ar_kernel(t_ref, o_ref, tbuf, hb, lb, gp, ra, aa, rb, ab, rc, ac, tsem, sa, qa, sb, qb, sc, qc, sd, qd, se, qe):
    gx = lax.axis_index("gx")
    gy = lax.axis_index("gy")
    x, y, z, c = gx // 4, gx % 4, gy // 2, gy % 2
    mate = z * 2 + 1 - c

    def plane(k, sign):
        dx, dy = OFFS[k]
        return ((x + sign * dx + 4) % 4) * 4 + (y + sign * dy + 4) % 4

    loads = [pltpu.make_async_copy(t_ref.at[pl.ds(4 * i, 4)], tbuf.at[pl.ds(4 * i, 4)], tsem.at[i]) for i in range(4)]
    for cp in loads:
        cp.start()
    barrier = pltpu.get_barrier_semaphore()
    pl.semaphore_signal(barrier, inc=1, device_id=(gx, mate), device_id_type=MESH)
    for k in range(15):
        pl.semaphore_signal(barrier, inc=1, device_id=(plane(k, 1), gy), device_id_type=MESH)
    for d in range(1, 4):
        pl.semaphore_signal(barrier, inc=1, device_id=(gx, ((z + d) % 4) * 2 + c), device_id_type=MESH)

    for i in range(4):
        loads[i].wait()
        for s in range(4 * i, 4 * i + 4):
            v = tbuf[s]
            h = v.astype(BF)
            hb[:, 128 * s:128 * s + 128] = h
            lb[:, 128 * s:128 * s + 128] = (v - h.astype(jnp.float32)).astype(BF)

    def dot(a, b):
        return lax.dot_general(a, b, NT, preferred_element_type=jnp.float32)

    for (r0, c0) in ((0, 0), (256, 0), (256, 256)):
        hr, lr = hb[r0:r0 + 256, :], lb[r0:r0 + 256, :]
        hc, lc = hb[c0:c0 + 256, :], lb[c0:c0 + 256, :]
        g = dot(hr, hc) + dot(hr, lc) + dot(lr, hc)
        for n, (i, j) in enumerate(BLOCKS):
            if r0 <= 128 * i < r0 + 256 and c0 <= 128 * j < c0 + 256:
                gp[16 * n:16 * n + 16] = g[128 * i - r0:128 * i - r0 + 128, 128 * j - c0:128 * j - c0 + 128].reshape(16, 8, 128)

    pl.semaphore_wait(barrier, 19)
    pieces = lambda core, g: pl.ds(80 * core + 5 * g, 5)

    def remote(src, dst, ss, rs, dev):
        return pltpu.make_async_remote_copy(src_ref=src, dst_ref=dst, send_sem=ss, recv_sem=rs, device_id=dev, device_id_type=MESH)

    A = [remote(gp.at[pieces(1 - c, plane(k, 1))], ra.at[k], sa.at[k], qa.at[k], (gx, mate)) for k in range(16)]
    for cp in A:
        cp.start()
    B = []
    for k in range(16):
        A[k].wait_recv()
        aa[k] = gp[pieces(c, plane(k, 1))] + ra[k]
        if k != SELF:
            cp = remote(aa.at[k], rb.at[k], sb.at[k], qb.at[k], (plane(k, 1), gy))
            cp.start()
            B.append(cp)
    total = aa[SELF]
    for k in range(14, -1, -1):
        B[k].wait_recv()
        total = total + rb[k]
    ab[...] = total
    rc[z] = total
    C = []
    for d in range(1, 4):
        cp = remote(ab, rc.at[z], sc.at[d], qc.at[d], (gx, ((z + d) % 4) * 2 + c))
        cp.start()
        C.append(cp)
    for cp in C:
        cp.wait_recv()
    total = (rc[0] + rc[1]) + (rc[2] + rc[3])
    ac[...] = total
    mine = pieces(c, gx)
    D = []
    for k in range(15):
        cp = remote(ac, o_ref.at[mine], sd.at[k], qd.at[k], (plane(k, 1), gy))
        cp.start()
        D.append(cp)
    o_ref[mine] = total
    E = [remote(ac, o_ref.at[mine], se.at[SELF], qe.at[SELF], (gx, mate))]
    E[0].start()
    for k in range(14, -1, -1):
        D[k].wait_recv()
        spot = pieces(c, plane(k, -1))
        cp = remote(o_ref.at[spot], o_ref.at[spot], se.at[k], qe.at[k], (gx, mate))
        cp.start()
        E.append(cp)
    for cp in E:
        cp.wait_recv()
    for cp in A + B + C + D + E:
        cp.wait_send()


def gram_sum(tensor):
    f = jnp.float32
    V, D = pltpu.VMEM, pltpu.SemaphoreType.DMA
    return pl.pallas_call(
        ar_kernel,
        out_shape=jax.ShapeDtypeStruct((160, 8, 128), f),
        in_specs=[pl.BlockSpec(memory_space=pl.ANY)],
        out_specs=pl.BlockSpec(memory_space=pltpu.VMEM),
        scratch_shapes=[
            V((16, 512, 128), f), V((512, 2048), BF), V((512, 2048), BF),
            V((160, 8, 128), f), V((16, 5, 8, 128), f), V((16, 5, 8, 128), f), V((16, 5, 8, 128), f),
            V((5, 8, 128), f), V((4, 5, 8, 128), f), V((5, 8, 128), f),
            D((4,)), D((16,)), D((16,)), D((16,)), D((16,)), D((4,)), D((4,)), D((16,)), D((16,)), D((16,)), D((16,)),
        ],
        compiler_params=pltpu.CompilerParams(collective_id=0, has_side_effects=True, vmem_limit_bytes=60 << 20),
        name="gram_sum",
    )(tensor)


def split(x):
    h = x.astype(jnp.bfloat16)
    return h, (x - h.astype(jnp.float32)).astype(jnp.bfloat16)


def mm(a, b, ca=1, cb=0):
    ah, al = split(a)
    bh, bl = split(b)

    def dot(u, v):
        return lax.dot_general(u, v, (((ca,), (cb,)), ((), ())), preferred_element_type=jnp.float32)

    return dot(ah, bh) + (dot(ah, bl) + dot(al, bh))


LOOK = 2


def lanes(x, i):
    return jnp.broadcast_to(x[:, i:i + 1], (8, 128))


def rows(x, i):
    return jnp.broadcast_to(x[i:i + 1, :], (8, 128))


def chol_inv(A, one):
    A = list(A)
    row = lax.broadcasted_iota(jnp.int32, (8, 128), 0)
    lane = lax.broadcasted_iota(jnp.int32, (8, 128), 1)
    out = []
    C = [lanes(A[0], j) * one for j in range(8)]
    for p in range(16):
        c = 8 * p
        done = (lane >= c) & (lane < c + 8)
        S = [[rows(C[j], i) for j in range(i + 1)] for i in range(8)]
        top = jnp.where(done, jnp.where(lane == row + c, 1.0, 0.0), A[p])
        V = [rows(top, i) for i in range(8)]
        near = range(p + 1, min(p + 1 + LOOK, 16))
        if p < 15:
            C = [lanes(A[p + 1], c + 8 + j) for j in range(8)]
        X = {g: [lanes(A[g], c + j) for j in range(8)] for g in range(p + 1, 16)}
        for g in range(p + 1, 16):
            A[g] = jnp.where(done, 0.0, A[g])
        L = [[None] * 8 for _ in range(8)]
        r = [None] * 8
        for j in range(8):
            r[j] = lax.rsqrt(S[j][j])
            for i in range(j + 1, 8):
                L[i][j] = S[i][j] * r[j]
            for i in range(j + 1, 8):
                for k in range(j + 1, i + 1):
                    S[i][k] = S[i][k] - L[i][j] * L[k][j]
            V[j] = V[j] * r[j]
            for g in near:
                x = X[g][j] * r[j]
                for k in range(j + 1, 8):
                    X[g][k] = X[g][k] - x * L[k][j]
                A[g] = A[g] - x * V[j]
                if g == p + 1:
                    for k in range(8):
                        C[k] = C[k] - x * rows(x, k)
            for i in range(j + 1, 8):
                V[i] = V[i] - L[i][j] * V[j]
        o = V[0]
        for i in range(1, 8):
            o = jnp.where(row == i, V[i], o)
        out.append(jnp.where(lane < c + 8, o, 0.0))
        if p + 1 + LOOK >= 16:
            continue
        F = list(V)
        for j in range(7, -1, -1):
            F[j] = F[j] * r[j]
            for i in range(j):
                F[i] = F[i] - L[j][i] * F[j]
        for g in range(p + 1 + LOOK, 16):
            t = [X[g][j] * F[j] for j in range(8)]
            t = [t[0] + t[1], t[2] + t[3], t[4] + t[5], t[6] + t[7]]
            A[g] = A[g] - ((t[0] + t[1]) + (t[2] + t[3]))
    return out


def sweep(pt, a, o_ref, li, one_ref):
    one_ref[...] = jnp.ones((8, 128), jnp.float32)
    a[...] = mm(pt[...], pt[...], 1, 1)

    def block(kb, _):
        k0 = pl.multiple_of(kb * 128, 128)
        Li = chol_inv([a[pl.ds(k0 + 8 * g, 8), pl.ds(k0, 128)] for g in range(16)], one_ref[...])
        for g in range(16):
            li[8 * g:8 * g + 8, :] = Li[g]
        for n in range(3):
            @pl.when(kb == n)
            def _():
                lo, hi = 128 * n, 128 * n + 128
                Q = mm(li[...], pt[lo:hi, :])
                o_ref[lo:hi, :] = Q
                if n < 2:
                    R = mm(li[...], a[lo:hi, hi:])
                    a[hi:, hi:] -= mm(R, R, 0, 0)
                    pt[hi:, :] -= mm(R, Q, 0, 0)
        return 0

    lax.fori_loop(0, 3, block, 0)


def first_kernel(p_ref, b_ref, g_ref, o_ref, pt, a, li, one):
    n = 0
    for i in range(4):
        for j in range(i + 1):
            blk = p_ref[16 * n:16 * n + 16].reshape(128, 128)
            g_ref[128 * i:128 * i + 128, 128 * j:128 * j + 128] = blk
            if j < i:
                g_ref[128 * j:128 * j + 128, 128 * i:128 * i + 128] = blk.T
            n += 1
    pt[...] = mm(b_ref[...], g_ref[...], 0, 0)
    sweep(pt, a, o_ref, li, one)


def second_kernel(g_ref, q_ref, o_ref, pt, a, li, one):
    pt[...] = mm(q_ref[...], g_ref[...])
    sweep(pt, a, o_ref, li, one)


SCRATCH = [pltpu.VMEM((384, 512), jnp.float32), pltpu.VMEM((384, 384), jnp.float32), pltpu.VMEM((128, 128), jnp.float32), pltpu.VMEM((8, 128), jnp.float32)]
WHOLE = pl.BlockSpec(memory_space=pltpu.VMEM)
SMALL = pltpu.CompilerParams(vmem_limit_bytes=16 << 20)
COST = pl.CostEstimate(flops=2000000000, bytes_accessed=3000000, transcendentals=0)


def sweep_first(packed, start):
    return pl.pallas_call(
        first_kernel,
        out_shape=(jax.ShapeDtypeStruct((512, 512), jnp.float32), jax.ShapeDtypeStruct((384, 512), jnp.float32)),
        in_specs=[WHOLE] * 2, out_specs=(WHOLE, WHOLE), scratch_shapes=SCRATCH, cost_estimate=COST, compiler_params=SMALL, name="sweep_first",
    )(packed, start)


def sweep_second(gram, basis_t):
    return pl.pallas_call(
        second_kernel,
        out_shape=jax.ShapeDtypeStruct((384, 512), jnp.float32),
        in_specs=[WHOLE] * 2, out_specs=WHOLE, scratch_shapes=SCRATCH, cost_estimate=COST, compiler_params=SMALL, name="sweep_second",
    )(gram, basis_t)


RELS = [(2, 0), (2, 1), (1, 0), (3, 0), (1, 1), (3, 1), (0, 1)]
GROUPS = [(0, 2), (2, 4), (4, 8), (8, 12), (12, 16)]


def core_kernel(q_ref, t_ref, o_ref, tbuf, qh, ql, y, tsem, ssem, rsem, osem):
    gx = lax.axis_index("gx")
    gy = lax.axis_index("gy")
    z, c = gy // 2, gy % 2

    def other(r):
        dz, dc = RELS[r]
        return ((z + dz) % 4) * 2 + (c + dc) % 2

    loads = [pltpu.make_async_copy(t_ref.at[pl.ds(a, b - a)], tbuf.at[pl.ds(a, b - a)], tsem.at[n]) for n, (a, b) in enumerate(GROUPS)]
    for cp in loads:
        cp.start()
    barrier = pltpu.get_barrier_semaphore()
    for r in range(7):
        pl.semaphore_signal(barrier, inc=1, device_id=(gx, other(r)), device_id_type=pl.DeviceIdType.MESH)
    v = q_ref[...]
    h = v.astype(jnp.bfloat16)
    qh[...] = h
    ql[...] = (v - h.astype(jnp.float32)).astype(jnp.bfloat16)

    def dot(a, b):
        return jnp.dot(a, b, preferred_element_type=jnp.float32)

    spot = pl.ds(pl.multiple_of(gy * 128, 128), 128)
    sends = []
    for n, (a, b) in enumerate(GROUPS):
        loads[n].wait()
        for k in range(a, b, 2):
            v = jnp.concatenate([tbuf[k], tbuf[k + 1]], axis=1)
            th = v.astype(jnp.bfloat16)
            tl = (v - th.astype(jnp.float32)).astype(jnp.bfloat16)
            out = dot(qh[...], th) + dot(qh[...], tl) + dot(ql[...], th)
            y[k] = out[:, :128]
            y[k + 1] = out[:, 128:]
        if n == 0:
            pl.semaphore_wait(barrier, 7)
        for r in range(7):
            cp = pltpu.make_async_remote_copy(
                src_ref=y.at[pl.ds(a, b - a), pl.ds(pl.multiple_of(48 * other(r), 8), 48)],
                dst_ref=o_ref.at[pl.ds(a, b - a), pl.ds(0, 48), spot],
                send_sem=ssem.at[r, n], recv_sem=rsem.at[r, n],
                device_id=(gx, other(r)), device_id_type=pl.DeviceIdType.MESH)
            cp.start()
            sends.append(cp)
    own = pltpu.make_async_copy(y.at[pl.ds(0, 16), pl.ds(pl.multiple_of(48 * gy, 8), 48)], o_ref.at[pl.ds(0, 16), pl.ds(0, 48), spot], osem)
    own.start()
    for cp in sends:
        cp.wait()
    own.wait()


def core_out(basis_t, tensor):
    f = jnp.float32
    V, D = pltpu.VMEM, pltpu.SemaphoreType.DMA
    ng = len(GROUPS)
    return pl.pallas_call(
        core_kernel,
        out_shape=jax.ShapeDtypeStruct((16, 48, 1024), f),
        in_specs=[pl.BlockSpec(memory_space=pltpu.VMEM), pl.BlockSpec(memory_space=pl.ANY)],
        out_specs=pl.BlockSpec(memory_space=pltpu.VMEM),
        scratch_shapes=[V((16, 512, 128), f), V((384, 512), jnp.bfloat16), V((384, 512), jnp.bfloat16), V((16, 384, 128), f),
                        D((ng,)), D((7, ng)), D((7, ng)), D],
        compiler_params=pltpu.CompilerParams(collective_id=1, has_side_effects=True, vmem_limit_bytes=24 << 20),
        name="core_out",
    )(basis_t, tensor)


def body(tensor, start_basis):
    gram, basis_t = sweep_first(gram_sum(tensor), start_basis)
    basis_t = sweep_second(gram, basis_t)
    return core_out(basis_t, tensor)


def solution(mesh):
    placed = (P("gx", None, "gy"), P())
    return jax.shard_map(
        body, mesh=mesh, in_specs=placed, out_specs=P("gx", "gy", None), check_vma=False
    )
```

```python
import jax
import jax.numpy as jnp
from jax import lax
from jax.experimental import pallas as pl
from jax.experimental.pallas import tpu as pltpu
from jax.sharding import PartitionSpec as P
MESH = pl.DeviceIdType.MESH
BF = jnp.bfloat16
BLOCKS = [(i, j) for i in range(4) for j in range(i + 1)]
OFFS = sorted(((dx, dy) for dx in range(4) for dy in range(4)), key=lambda o: -(min(o[0], 4 - o[0]) + min(o[1], 4 - o[1])))
SELF = 15
NT = (((1,), (1,)), ((), ()))


def ar_kernel(t_ref, o_ref, tbuf, hb, lb, gp, ra, aa, rb, ab, rc, ac, tsem, sa, qa, sb, qb, sc, qc, sd, qd, se, qe):
    gx = lax.axis_index("gx")
    gy = lax.axis_index("gy")
    x, y, z, c = gx // 4, gx % 4, gy // 2, gy % 2
    mate = z * 2 + 1 - c

    def plane(k, sign):
        dx, dy = OFFS[k]
        return ((x + sign * dx + 4) % 4) * 4 + (y + sign * dy + 4) % 4

    loads = [pltpu.make_async_copy(t_ref.at[pl.ds(4 * i, 4)], tbuf.at[pl.ds(4 * i, 4)], tsem.at[i]) for i in range(4)]
    for cp in loads:
        cp.start()
    barrier = pltpu.get_barrier_semaphore()
    pl.semaphore_signal(barrier, inc=1, device_id=(gx, mate), device_id_type=MESH)
    for k in range(15):
        pl.semaphore_signal(barrier, inc=1, device_id=(plane(k, 1), gy), device_id_type=MESH)
    for d in range(1, 4):
        pl.semaphore_signal(barrier, inc=1, device_id=(gx, ((z + d) % 4) * 2 + c), device_id_type=MESH)

    def dot(a, b):
        return lax.dot_general(a, b, NT, preferred_element_type=jnp.float32)

    for i in range(4):
        loads[i].wait()
        for s in range(4 * i, 4 * i + 4):
            v = tbuf[s]
            h = v.astype(BF)
            hb[:, 128 * s:128 * s + 128] = h
            lb[:, 128 * s:128 * s + 128] = (v - h.astype(jnp.float32)).astype(BF)
        if i % 2 == 0:
            continue
        ks = slice(1024 * (i // 2), 1024 * (i // 2) + 1024)
        for (r0, c0) in ((0, 0), (256, 0), (256, 256)):
            hr, lr = hb[r0:r0 + 256, ks], lb[r0:r0 + 256, ks]
            hc, lc = hb[c0:c0 + 256, ks], lb[c0:c0 + 256, ks]
            g = dot(hr, hc) + dot(hr, lc) + dot(lr, hc)
            for n, (bi, bj) in enumerate(BLOCKS):
                if r0 <= 128 * bi < r0 + 256 and c0 <= 128 * bj < c0 + 256:
                    part = g[128 * bi - r0:128 * bi - r0 + 128, 128 * bj - c0:128 * bj - c0 + 128].reshape(16, 8, 128)
                    if i == 1:
                        gp[16 * n:16 * n + 16] = part
                    else:
                        gp[16 * n:16 * n + 16] += part

    pl.semaphore_wait(barrier, 19)
    pieces = lambda core, g: pl.ds(80 * core + 5 * g, 5)

    def remote(src, dst, ss, rs, dev):
        return pltpu.make_async_remote_copy(src_ref=src, dst_ref=dst, send_sem=ss, recv_sem=rs, device_id=dev, device_id_type=MESH)

    A = [remote(gp.at[pieces(1 - c, plane(k, 1))], ra.at[k], sa.at[k], qa.at[k], (gx, mate)) for k in range(16)]
    for cp in A:
        cp.start()
    B = []
    for k in range(16):
        A[k].wait_recv()
        aa[k] = gp[pieces(c, plane(k, 1))] + ra[k]
        if k != SELF:
            cp = remote(aa.at[k], rb.at[k], sb.at[k], qb.at[k], (plane(k, 1), gy))
            cp.start()
            B.append(cp)
    total = aa[SELF]
    for k in range(14, -1, -1):
        B[k].wait_recv()
        total = total + rb[k]
    ab[...] = total
    rc[z] = total
    C = []
    for d in range(1, 4):
        cp = remote(ab, rc.at[z], sc.at[d], qc.at[d], (gx, ((z + d) % 4) * 2 + c))
        cp.start()
        C.append(cp)
    for cp in C:
        cp.wait_recv()
    total = (rc[0] + rc[1]) + (rc[2] + rc[3])
    ac[...] = total
    mine = pieces(c, gx)
    D = []
    for k in range(15):
        cp = remote(ac, o_ref.at[mine], sd.at[k], qd.at[k], (plane(k, 1), gy))
        cp.start()
        D.append(cp)
    o_ref[mine] = total
    E = [remote(ac, o_ref.at[mine], se.at[SELF], qe.at[SELF], (gx, mate))]
    E[0].start()
    for k in range(14, -1, -1):
        D[k].wait_recv()
        spot = pieces(c, plane(k, -1))
        cp = remote(o_ref.at[spot], o_ref.at[spot], se.at[k], qe.at[k], (gx, mate))
        cp.start()
        E.append(cp)
    for cp in E:
        cp.wait_recv()
    for cp in A + B + C + D + E:
        cp.wait_send()


def gram_sum(tensor):
    f = jnp.float32
    V, D = pltpu.VMEM, pltpu.SemaphoreType.DMA
    return pl.pallas_call(
        ar_kernel,
        out_shape=jax.ShapeDtypeStruct((160, 8, 128), f),
        in_specs=[pl.BlockSpec(memory_space=pl.ANY)],
        out_specs=pl.BlockSpec(memory_space=pltpu.VMEM),
        scratch_shapes=[
            V((16, 512, 128), f), V((512, 2048), BF), V((512, 2048), BF),
            V((160, 8, 128), f), V((16, 5, 8, 128), f), V((16, 5, 8, 128), f), V((16, 5, 8, 128), f),
            V((5, 8, 128), f), V((4, 5, 8, 128), f), V((5, 8, 128), f),
            D((4,)), D((16,)), D((16,)), D((16,)), D((16,)), D((4,)), D((4,)), D((16,)), D((16,)), D((16,)), D((16,)),
        ],
        compiler_params=pltpu.CompilerParams(collective_id=0, has_side_effects=True, vmem_limit_bytes=60 << 20),
        name="gram_sum",
    )(tensor)


def split(x):
    h = x.astype(jnp.bfloat16)
    return h, (x - h.astype(jnp.float32)).astype(jnp.bfloat16)


def mm(a, b, ca=1, cb=0):
    ah, al = split(a)
    bh, bl = split(b)

    def dot(u, v):
        return lax.dot_general(u, v, (((ca,), (cb,)), ((), ())), preferred_element_type=jnp.float32)

    return dot(ah, bh) + (dot(ah, bl) + dot(al, bh))


LOOK = 2


def lanes(x, i):
    return jnp.broadcast_to(x[:, i:i + 1], (8, 128))


def rows(x, i):
    return jnp.broadcast_to(x[i:i + 1, :], (8, 128))


def chol_steps(A, one, li):
    row = lax.broadcasted_iota(jnp.int32, (8, 128), 0)
    lane = lax.broadcasted_iota(jnp.int32, (8, 128), 1)
    C = [lanes(A[0], j) * one for j in range(8)]
    for p in range(16):
        c = 8 * p
        done = (lane >= c) & (lane < c + 8)
        S = [[rows(C[j], i) for j in range(i + 1)] for i in range(8)]
        top = jnp.where(done, jnp.where(lane == row + c, 1.0, 0.0), A[p])
        V = [rows(top, i) for i in range(8)]
        near = range(p + 1, min(p + 1 + LOOK, 16))
        if p < 15:
            C = [lanes(A[p + 1], c + 8 + j) for j in range(8)]
        X = {g: [lanes(A[g], c + j) for j in range(8)] for g in range(p + 1, 16)}
        for g in range(p + 1, 16):
            A[g] = jnp.where(done, 0.0, A[g])
        L = [[None] * 8 for _ in range(8)]
        r = [None] * 8
        for j in range(8):
            r[j] = lax.rsqrt(S[j][j])
            for i in range(j + 1, 8):
                L[i][j] = S[i][j] * r[j]
            for i in range(j + 1, 8):
                for k in range(j + 1, i + 1):
                    S[i][k] = S[i][k] - L[i][j] * L[k][j]
            V[j] = V[j] * r[j]
            for g in near:
                x = X[g][j] * r[j]
                for k in range(j + 1, 8):
                    X[g][k] = X[g][k] - x * L[k][j]
                A[g] = A[g] - x * V[j]
                if g == p + 1:
                    for k in range(8):
                        C[k] = C[k] - x * rows(x, k)
            for i in range(j + 1, 8):
                V[i] = V[i] - L[i][j] * V[j]
        o = V[0]
        for i in range(1, 8):
            o = jnp.where(row == i, V[i], o)
        li[c:c + 8, :] = jnp.where(lane < c + 8, o, 0.0)
        yield
        if p + 1 + LOOK >= 16:
            continue
        F = list(V)
        for j in range(7, -1, -1):
            F[j] = F[j] * r[j]
            for i in range(j):
                F[i] = F[i] - L[j][i] * F[j]
        for g in range(p + 1 + LOOK, 16):
            t = [X[g][j] * F[j] for j in range(8)]
            t = [t[0] + t[1], t[2] + t[3], t[4] + t[5], t[6] + t[7]]
            A[g] = A[g] - ((t[0] + t[1]) + (t[2] + t[3]))


def groups(ref):
    return [ref[8 * g:8 * g + 8, :] for g in range(16)]


def run(*steps):
    steps = list(steps)
    while steps:
        for one in list(steps):
            if next(one, True) is True:
                steps.remove(one)


def sweeps_kernel(p_ref, b_ref, o_ref, g_ref, p, q, a, li, one_ref):
    n = 0
    for i in range(4):
        for j in range(i + 1):
            blk = p_ref[16 * n:16 * n + 16].reshape(128, 128)
            g_ref[128 * i:128 * i + 128, 128 * j:128 * j + 128] = blk
            if j < i:
                g_ref[128 * j:128 * j + 128, 128 * i:128 * i + 128] = blk.T
            n += 1
    one_ref[...] = jnp.ones((8, 128), jnp.float32)
    one = one_ref[...]
    first, second = 0, 3

    def product(s, k, source, cs):
        p[s + k] = mm(source, g_ref[...], cs, 0)
        for j in range(k + 1):
            a[s + j, k] = mm(p[s + j], p[s + k], 1, 1)

    def basis(s, k):
        q[s + k] = mm(li[s + k], p[s + k])

    def factor(s, k, j):
        a[s + k, j] = mm(li[s + k], a[s + k, j])

    def reduce_gram(s, k, i, j):
        a[s + i, j] -= mm(a[s + k, i], a[s + k, j], 0, 0)

    def reduce_product(s, k, j):
        p[s + j] -= mm(a[s + k, j], q[s + k], 0, 0)

    def chol(s, k):
        return chol_steps(groups(a.at[s + k, k]), one, li.at[s + k])

    for k in range(3):
        product(first, k, b_ref[:, 128 * k:128 * k + 128], 0)
    run(chol(first, 0))
    factor(first, 0, 1)
    reduce_gram(first, 0, 1, 1)
    basis(first, 0)
    product(second, 0, q[0], 1)
    factor(first, 0, 2)
    reduce_gram(first, 0, 1, 2)
    reduce_gram(first, 0, 2, 2)
    reduce_product(first, 0, 1)
    reduce_product(first, 0, 2)
    run(chol(first, 1), chol(second, 0))
    factor(first, 1, 2)
    reduce_gram(first, 1, 2, 2)
    basis(first, 1)
    product(second, 1, q[1], 1)
    factor(second, 0, 1)
    reduce_gram(second, 0, 1, 1)
    reduce_product(first, 1, 2)
    basis(second, 0)
    reduce_product(second, 0, 1)
    run(chol(first, 2), chol(second, 1))
    basis(first, 2)
    product(second, 2, q[2], 1)
    factor(second, 0, 2)
    reduce_gram(second, 0, 2, 2)
    factor(second, 1, 2)
    reduce_gram(second, 1, 2, 2)
    basis(second, 1)
    reduce_product(second, 0, 2)
    reduce_product(second, 1, 2)
    run(chol(second, 2))
    basis(second, 2)
    for k in range(3):
        o_ref[128 * k:128 * k + 128, :] = q[3 + k]


def sweeps(packed, start):
    f = jnp.float32
    whole = pl.BlockSpec(memory_space=pltpu.VMEM)
    return pl.pallas_call(
        sweeps_kernel,
        out_shape=jax.ShapeDtypeStruct((384, 512), f),
        in_specs=[whole] * 2, out_specs=whole,
        scratch_shapes=[pltpu.VMEM((512, 512), f), pltpu.VMEM((6, 128, 512), f), pltpu.VMEM((6, 128, 512), f),
                        pltpu.VMEM((6, 3, 128, 128), f), pltpu.VMEM((6, 128, 128), f), pltpu.VMEM((8, 128), f)],
        cost_estimate=pl.CostEstimate(flops=4000000000, bytes_accessed=3000000, transcendentals=0),
        compiler_params=pltpu.CompilerParams(vmem_limit_bytes=24 << 20), name="sweeps",
    )(packed, start)


RELS = [(2, 0), (2, 1), (1, 0), (3, 0), (1, 1), (3, 1), (0, 1)]
GROUPS = [(0, 2), (2, 4), (4, 8), (8, 12), (12, 16)]


def core_kernel(q_ref, t_ref, o_ref, tbuf, qh, ql, y, tsem, ssem, rsem, osem):
    gx = lax.axis_index("gx")
    gy = lax.axis_index("gy")
    z, c = gy // 2, gy % 2

    def other(r):
        dz, dc = RELS[r]
        return ((z + dz) % 4) * 2 + (c + dc) % 2

    loads = [pltpu.make_async_copy(t_ref.at[pl.ds(a, b - a)], tbuf.at[pl.ds(a, b - a)], tsem.at[n]) for n, (a, b) in enumerate(GROUPS)]
    for cp in loads:
        cp.start()
    barrier = pltpu.get_barrier_semaphore()
    for r in range(7):
        pl.semaphore_signal(barrier, inc=1, device_id=(gx, other(r)), device_id_type=pl.DeviceIdType.MESH)
    v = q_ref[...]
    h = v.astype(jnp.bfloat16)
    qh[...] = h
    ql[...] = (v - h.astype(jnp.float32)).astype(jnp.bfloat16)

    def dot(a, b):
        return jnp.dot(a, b, preferred_element_type=jnp.float32)

    spot = pl.ds(pl.multiple_of(gy * 128, 128), 128)
    sends = []
    for n, (a, b) in enumerate(GROUPS):
        loads[n].wait()
        for k in range(a, b, 2):
            v = jnp.concatenate([tbuf[k], tbuf[k + 1]], axis=1)
            th = v.astype(jnp.bfloat16)
            tl = (v - th.astype(jnp.float32)).astype(jnp.bfloat16)
            out = dot(qh[...], th) + dot(qh[...], tl) + dot(ql[...], th)
            y[k] = out[:, :128]
            y[k + 1] = out[:, 128:]
        if n == 0:
            pl.semaphore_wait(barrier, 7)
        for r in range(7):
            cp = pltpu.make_async_remote_copy(
                src_ref=y.at[pl.ds(a, b - a), pl.ds(pl.multiple_of(48 * other(r), 8), 48)],
                dst_ref=o_ref.at[pl.ds(a, b - a), pl.ds(0, 48), spot],
                send_sem=ssem.at[r, n], recv_sem=rsem.at[r, n],
                device_id=(gx, other(r)), device_id_type=pl.DeviceIdType.MESH)
            cp.start()
            sends.append(cp)
    own = pltpu.make_async_copy(y.at[pl.ds(0, 16), pl.ds(pl.multiple_of(48 * gy, 8), 48)], o_ref.at[pl.ds(0, 16), pl.ds(0, 48), spot], osem)
    own.start()
    for cp in sends:
        cp.wait()
    own.wait()


def core_out(basis_t, tensor):
    f = jnp.float32
    V, D = pltpu.VMEM, pltpu.SemaphoreType.DMA
    ng = len(GROUPS)
    return pl.pallas_call(
        core_kernel,
        out_shape=jax.ShapeDtypeStruct((16, 48, 1024), f),
        in_specs=[pl.BlockSpec(memory_space=pltpu.VMEM), pl.BlockSpec(memory_space=pl.ANY)],
        out_specs=pl.BlockSpec(memory_space=pltpu.VMEM),
        scratch_shapes=[V((16, 512, 128), f), V((384, 512), jnp.bfloat16), V((384, 512), jnp.bfloat16), V((16, 384, 128), f),
                        D((ng,)), D((7, ng)), D((7, ng)), D],
        compiler_params=pltpu.CompilerParams(collective_id=1, has_side_effects=True, vmem_limit_bytes=24 << 20),
        name="core_out",
    )(basis_t, tensor)


def body(tensor, start_basis):
    return core_out(sweeps(gram_sum(tensor), start_basis), tensor)


def solution(mesh):
    placed = (P("gx", None, "gy"), P())
    return jax.shard_map(
        body, mesh=mesh, in_specs=placed, out_specs=P("gx", "gy", None), check_vma=False
    )
```

```python
import jax
import jax.numpy as jnp
from jax import lax
from jax.experimental import pallas as pl
from jax.experimental.pallas import tpu as pltpu
from jax.sharding import PartitionSpec as P
MESH = pl.DeviceIdType.MESH
BF = jnp.bfloat16
BLOCKS = [(i, j) for i in range(4) for j in range(i + 1)]
OFFS = sorted(((dx, dy) for dx in range(4) for dy in range(4)), key=lambda o: -(min(o[0], 4 - o[0]) + min(o[1], 4 - o[1])))
SELF = 15
NT = (((1,), (1,)), ((), ()))


def ar_kernel(t_ref, o_ref, early_ref, tbuf, hb, lb, gp, ra, aa, rb, ab, rc, ac, tsem, sa, qa, sb, qb, sc, qc, sd, qd, se, qe, esem):
    gx = lax.axis_index("gx")
    gy = lax.axis_index("gy")
    x, y, z, c = gx // 4, gx % 4, gy // 2, gy % 2
    mate = z * 2 + 1 - c

    def plane(k, sign):
        dx, dy = OFFS[k]
        return ((x + sign * dx + 4) % 4) * 4 + (y + sign * dy + 4) % 4

    loads = [pltpu.make_async_copy(t_ref.at[pl.ds(4 * i, 4)], tbuf.at[pl.ds(4 * i, 4)], tsem.at[i]) for i in range(4)]
    for cp in loads:
        cp.start()
    barrier = pltpu.get_barrier_semaphore()
    pl.semaphore_signal(barrier, inc=1, device_id=(gx, mate), device_id_type=MESH)
    for k in range(15):
        pl.semaphore_signal(barrier, inc=1, device_id=(plane(k, 1), gy), device_id_type=MESH)
    for d in range(1, 4):
        pl.semaphore_signal(barrier, inc=1, device_id=(gx, ((z + d) % 4) * 2 + c), device_id_type=MESH)

    for i in range(4):
        loads[i].wait()
        for s in range(4 * i, 4 * i + 4):
            v = tbuf[s]
            h = v.astype(BF)
            hb[:, 128 * s:128 * s + 128] = h
            lb[:, 128 * s:128 * s + 128] = (v - h.astype(jnp.float32)).astype(BF)

    keep = pltpu.make_async_copy(tbuf.at[pl.ds(0, KG)], early_ref, esem)
    keep.start()

    def dot(a, b):
        return lax.dot_general(a, b, NT, preferred_element_type=jnp.float32)

    for (r0, c0) in ((0, 0), (256, 0), (256, 256)):
        hr, lr = hb[r0:r0 + 256, :], lb[r0:r0 + 256, :]
        hc, lc = hb[c0:c0 + 256, :], lb[c0:c0 + 256, :]
        g = dot(hr, hc) + dot(hr, lc) + dot(lr, hc)
        for n, (i, j) in enumerate(BLOCKS):
            if r0 <= 128 * i < r0 + 256 and c0 <= 128 * j < c0 + 256:
                gp[16 * n:16 * n + 16] = g[128 * i - r0:128 * i - r0 + 128, 128 * j - c0:128 * j - c0 + 128].reshape(16, 8, 128)

    pl.semaphore_wait(barrier, 19)
    pieces = lambda core, g: pl.ds(80 * core + 5 * g, 5)

    def remote(src, dst, ss, rs, dev):
        return pltpu.make_async_remote_copy(src_ref=src, dst_ref=dst, send_sem=ss, recv_sem=rs, device_id=dev, device_id_type=MESH)

    A = [remote(gp.at[pieces(1 - c, plane(k, 1))], ra.at[k], sa.at[k], qa.at[k], (gx, mate)) for k in range(16)]
    for cp in A:
        cp.start()
    B = []
    for k in range(16):
        A[k].wait_recv()
        aa[k] = gp[pieces(c, plane(k, 1))] + ra[k]
        if k != SELF:
            cp = remote(aa.at[k], rb.at[k], sb.at[k], qb.at[k], (plane(k, 1), gy))
            cp.start()
            B.append(cp)
    total = aa[SELF]
    for k in range(14, -1, -1):
        B[k].wait_recv()
        total = total + rb[k]
    ab[...] = total
    rc[z] = total
    C = []
    for d in range(1, 4):
        cp = remote(ab, rc.at[z], sc.at[d], qc.at[d], (gx, ((z + d) % 4) * 2 + c))
        cp.start()
        C.append(cp)
    for cp in C:
        cp.wait_recv()
    total = (rc[0] + rc[1]) + (rc[2] + rc[3])
    ac[...] = total
    mine = pieces(c, gx)
    D = []
    for k in range(15):
        cp = remote(ac, o_ref.at[mine], sd.at[k], qd.at[k], (plane(k, 1), gy))
        cp.start()
        D.append(cp)
    o_ref[mine] = total
    E = [remote(ac, o_ref.at[mine], se.at[SELF], qe.at[SELF], (gx, mate))]
    E[0].start()
    for k in range(14, -1, -1):
        D[k].wait_recv()
        spot = pieces(c, plane(k, -1))
        cp = remote(o_ref.at[spot], o_ref.at[spot], se.at[k], qe.at[k], (gx, mate))
        cp.start()
        E.append(cp)
    for cp in E:
        cp.wait_recv()
    keep.wait()
    for cp in A + B + C + D + E:
        cp.wait_send()


def gram_sum(tensor):
    f = jnp.float32
    V, D = pltpu.VMEM, pltpu.SemaphoreType.DMA
    return pl.pallas_call(
        ar_kernel,
        out_shape=(jax.ShapeDtypeStruct((160, 8, 128), f), jax.ShapeDtypeStruct((KG, 512, 128), f)),
        in_specs=[pl.BlockSpec(memory_space=pl.ANY)],
        out_specs=(pl.BlockSpec(memory_space=pltpu.VMEM), pl.BlockSpec(memory_space=pl.ANY)),
        scratch_shapes=[
            V((16, 512, 128), f), V((512, 2048), BF), V((512, 2048), BF),
            V((160, 8, 128), f), V((16, 5, 8, 128), f), V((16, 5, 8, 128), f), V((16, 5, 8, 128), f),
            V((5, 8, 128), f), V((4, 5, 8, 128), f), V((5, 8, 128), f),
            D((4,)), D((16,)), D((16,)), D((16,)), D((16,)), D((4,)), D((4,)), D((16,)), D((16,)), D((16,)), D((16,)), D,
        ],
        compiler_params=pltpu.CompilerParams(collective_id=0, has_side_effects=True, vmem_limit_bytes=60 << 20),
        name="gram_sum",
    )(tensor)


KG = 2


def split(x):
    h = x.astype(jnp.bfloat16)
    return h, (x - h.astype(jnp.float32)).astype(jnp.bfloat16)


def mm(a, b, ca=1, cb=0):
    ah, al = split(a)
    bh, bl = split(b)

    def dot(u, v):
        return lax.dot_general(u, v, (((ca,), (cb,)), ((), ())), preferred_element_type=jnp.float32)

    return dot(ah, bh) + (dot(ah, bl) + dot(al, bh))


LOOK = 2


def lanes(x, i):
    return jnp.broadcast_to(x[:, i:i + 1], (8, 128))


def rows(x, i):
    return jnp.broadcast_to(x[i:i + 1, :], (8, 128))


def chol_steps(A, one, li):
    row = lax.broadcasted_iota(jnp.int32, (8, 128), 0)
    lane = lax.broadcasted_iota(jnp.int32, (8, 128), 1)
    C = [lanes(A[0], j) * one for j in range(8)]
    for p in range(16):
        c = 8 * p
        done = (lane >= c) & (lane < c + 8)
        S = [[rows(C[j], i) for j in range(i + 1)] for i in range(8)]
        top = jnp.where(done, jnp.where(lane == row + c, 1.0, 0.0), A[p])
        V = [rows(top, i) for i in range(8)]
        near = range(p + 1, min(p + 1 + LOOK, 16))
        if p < 15:
            C = [lanes(A[p + 1], c + 8 + j) for j in range(8)]
        X = {g: [lanes(A[g], c + j) for j in range(8)] for g in range(p + 1, 16)}
        for g in range(p + 1, 16):
            A[g] = jnp.where(done, 0.0, A[g])
        L = [[None] * 8 for _ in range(8)]
        r = [None] * 8
        for j in range(8):
            r[j] = lax.rsqrt(S[j][j])
            for i in range(j + 1, 8):
                L[i][j] = S[i][j] * r[j]
            for i in range(j + 1, 8):
                for k in range(j + 1, i + 1):
                    S[i][k] = S[i][k] - L[i][j] * L[k][j]
            V[j] = V[j] * r[j]
            for g in near:
                x = X[g][j] * r[j]
                for k in range(j + 1, 8):
                    X[g][k] = X[g][k] - x * L[k][j]
                A[g] = A[g] - x * V[j]
                if g == p + 1:
                    for k in range(8):
                        C[k] = C[k] - x * rows(x, k)
            for i in range(j + 1, 8):
                V[i] = V[i] - L[i][j] * V[j]
        o = V[0]
        for i in range(1, 8):
            o = jnp.where(row == i, V[i], o)
        li[c:c + 8, :] = jnp.where(lane < c + 8, o, 0.0)
        yield
        if p + 1 + LOOK >= 16:
            continue
        F = list(V)
        for j in range(7, -1, -1):
            F[j] = F[j] * r[j]
            for i in range(j):
                F[i] = F[i] - L[j][i] * F[j]
        for g in range(p + 1 + LOOK, 16):
            t = [X[g][j] * F[j] for j in range(8)]
            t = [t[0] + t[1], t[2] + t[3], t[4] + t[5], t[6] + t[7]]
            A[g] = A[g] - ((t[0] + t[1]) + (t[2] + t[3]))


def groups(ref):
    return [ref[8 * g:8 * g + 8, :] for g in range(16)]


def run(*steps):
    steps = list(steps)
    while steps:
        for one in list(steps):
            if next(one, True) is True:
                steps.remove(one)


def sweeps_kernel(p_ref, b_ref, t_ref, o_ref, below, above, far, g_ref, p, q, a, li, one_ref, ssem, rsem):
    gx = lax.axis_index("gx")
    gy = lax.axis_index("gy")
    up, down = (gy + 2) % 8, (gy + 6) % 8
    barrier = pltpu.get_barrier_semaphore()
    for dev in (up, down):
        pl.semaphore_signal(barrier, inc=1, device_id=(gx, dev), device_id_type=pl.DeviceIdType.MESH)
    moves = []

    def move(src, dst, dev):
        n = len(moves)
        cp = pltpu.make_async_remote_copy(src_ref=src, dst_ref=dst, send_sem=ssem.at[n], recv_sem=rsem.at[n], device_id=(gx, dev), device_id_type=pl.DeviceIdType.MESH)
        cp.start()
        moves.append(cp)

    n = 0
    for i in range(4):
        for j in range(i + 1):
            blk = p_ref[16 * n:16 * n + 16].reshape(128, 128)
            g_ref[128 * i:128 * i + 128, 128 * j:128 * j + 128] = blk
            if j < i:
                g_ref[128 * j:128 * j + 128, 128 * i:128 * i + 128] = blk.T
            n += 1
    pl.semaphore_wait(barrier, 2)
    for n in range(KG):
        move(t_ref.at[n], below.at[n], up)
        move(t_ref.at[KG - 1 - n], above.at[KG - 1 - n], down)
    one_ref[...] = jnp.ones((8, 128), jnp.float32)
    one = one_ref[...]
    first, second = 0, 3

    def product(s, k, source, cs):
        p[s + k] = mm(source, g_ref[...], cs, 0)
        for j in range(k + 1):
            a[s + j, k] = mm(p[s + j], p[s + k], 1, 1)

    def basis(s, k):
        q[s + k] = mm(li[s + k], p[s + k])

    def factor(s, k, j):
        a[s + k, j] = mm(li[s + k], a[s + k, j])

    def reduce_gram(s, k, i, j):
        a[s + i, j] -= mm(a[s + k, i], a[s + k, j], 0, 0)

    def reduce_product(s, k, j):
        p[s + j] -= mm(a[s + k, j], q[s + k], 0, 0)

    def chol(s, k):
        return chol_steps(groups(a.at[s + k, k]), one, li.at[s + k])

    for k in range(3):
        product(first, k, b_ref[:, 128 * k:128 * k + 128], 0)
    run(chol(first, 0))
    factor(first, 0, 1)
    reduce_gram(first, 0, 1, 1)
    basis(first, 0)
    product(second, 0, q[0], 1)
    factor(first, 0, 2)
    reduce_gram(first, 0, 1, 2)
    reduce_gram(first, 0, 2, 2)
    reduce_product(first, 0, 1)
    reduce_product(first, 0, 2)
    run(chol(first, 1), chol(second, 0))
    factor(first, 1, 2)
    reduce_gram(first, 1, 2, 2)
    basis(first, 1)
    product(second, 1, q[1], 1)
    factor(second, 0, 1)
    reduce_gram(second, 0, 1, 1)
    reduce_product(first, 1, 2)
    basis(second, 0)
    reduce_product(second, 0, 1)
    for n in range(KG // 2):
        moves[2 * n].wait_recv()
        moves[2 * n + 1].wait_recv()
        move(below.at[n], far.at[n], up)
        move(above.at[KG - 1 - n], far.at[KG - 1 - n], down)
    run(chol(first, 2), chol(second, 1))
    basis(first, 2)
    product(second, 2, q[2], 1)
    factor(second, 0, 2)
    reduce_gram(second, 0, 2, 2)
    factor(second, 1, 2)
    reduce_gram(second, 1, 2, 2)
    basis(second, 1)
    reduce_product(second, 0, 2)
    reduce_product(second, 1, 2)
    run(chol(second, 2))
    basis(second, 2)
    for k in range(3):
        o_ref[128 * k:128 * k + 128, :] = q[3 + k]
    for n, cp in enumerate(moves):
        cp.wait_send()
        if n >= KG:
            cp.wait_recv()


def sweeps(packed, start, tensor):
    f = jnp.float32
    whole = pl.BlockSpec(memory_space=pltpu.VMEM)
    anywhere = pl.BlockSpec(memory_space=pl.ANY)
    return pl.pallas_call(
        sweeps_kernel,
        out_shape=(jax.ShapeDtypeStruct((384, 512), f),) + (jax.ShapeDtypeStruct((KG, 512, 128), f),) * 3,
        in_specs=[whole] * 2 + [anywhere], out_specs=(whole,) + (anywhere,) * 3,
        scratch_shapes=[pltpu.VMEM((512, 512), f), pltpu.VMEM((6, 128, 512), f), pltpu.VMEM((6, 128, 512), f),
                        pltpu.VMEM((6, 3, 128, 128), f), pltpu.VMEM((6, 128, 128), f), pltpu.VMEM((8, 128), f),
                        pltpu.SemaphoreType.DMA((3 * KG,)), pltpu.SemaphoreType.DMA((3 * KG,))],
        cost_estimate=pl.CostEstimate(flops=4000000000, bytes_accessed=3000000, transcendentals=0),
        compiler_params=pltpu.CompilerParams(collective_id=2, has_side_effects=True, vmem_limit_bytes=24 << 20), name="sweeps",
    )(packed, start, tensor)


RELS = [(2, 0), (2, 1), (1, 0), (3, 0), (1, 1), (3, 1), (0, 1)]
KG = 2
GROUPS = [(0, 2), (2, 4), (4, 8), (8, 14)]


def core_kernel(q_ref, t_ref, g1, g3, g2, o_ref, tbuf, gbuf, qh, ql, y, yg, tsem, gsem, ssem, rsem, xsem, wsem, osem):
    gx = lax.axis_index("gx")
    gy = lax.axis_index("gy")
    z, c = gy // 2, gy % 2

    def other(r):
        dz, dc = RELS[r]
        return ((z + dz) % 4) * 2 + (c + dc) % 2

    na = 16 - KG
    loads = [pltpu.make_async_copy(t_ref.at[pl.ds(KG + a, b - a)], tbuf.at[pl.ds(a, b - a)], tsem.at[n]) for n, (a, b) in enumerate(GROUPS)]
    gloads = [[pltpu.make_async_copy(r, gbuf.at[s], gsem.at[s])] for s, r in enumerate((t_ref.at[pl.ds(0, KG)], g1, g3, g2))]
    for cp in loads:
        cp.start()
    for cps in gloads:
        for cp in cps:
            cp.start()
    barrier = pltpu.get_barrier_semaphore()
    for r in range(7):
        pl.semaphore_signal(barrier, inc=1, device_id=(gx, other(r)), device_id_type=pl.DeviceIdType.MESH)
    v = q_ref[...]
    h = v.astype(jnp.bfloat16)
    qh[...] = h
    ql[...] = (v - h.astype(jnp.float32)).astype(jnp.bfloat16)

    def dot(a, b):
        return jnp.dot(a, b, preferred_element_type=jnp.float32)

    def split(v):
        th = v.astype(jnp.bfloat16)
        return th, (v - th.astype(jnp.float32)).astype(jnp.bfloat16)

    def cols(dev):
        return pl.ds(pl.multiple_of(dev * 128, 128), 128)

    sends = []
    for n, (a, b) in enumerate(GROUPS):
        loads[n].wait()
        for k in range(a, b, 2):
            th, tl = split(jnp.concatenate([tbuf[k], tbuf[k + 1]], axis=1))
            out = dot(qh[...], th) + dot(qh[...], tl) + dot(ql[...], th)
            y[k] = out[:, :128]
            y[k + 1] = out[:, 128:]
        if n == 0:
            pl.semaphore_wait(barrier, 7)
        for r in range(7):
            cp = pltpu.make_async_remote_copy(
                src_ref=y.at[pl.ds(a, b - a), pl.ds(pl.multiple_of(48 * other(r), 8), 48)],
                dst_ref=o_ref.at[pl.ds(KG + a, b - a), pl.ds(0, 48), cols(gy)],
                send_sem=ssem.at[r, n], recv_sem=rsem.at[r, n],
                device_id=(gx, other(r)), device_id_type=pl.DeviceIdType.MESH)
            cp.start()
            sends.append(cp)
    own = pltpu.make_async_copy(y.at[pl.ds(0, na), pl.ds(pl.multiple_of(48 * gy, 8), 48)], o_ref.at[pl.ds(KG, na), pl.ds(0, 48), cols(gy)], osem.at[4])
    own.start()
    rows = pl.ds(pl.multiple_of(96 * z, 32), 96)
    q2 = jnp.concatenate([qh[rows, :], ql[rows, :]], axis=0)
    locs = [own]
    for s, dz in enumerate((0, 3, 1, 2)):
        for cp in gloads[s]:
            cp.wait()
        for k in range(0, KG, 2):
            th, tl = split(jnp.concatenate([gbuf[s, k], gbuf[s, k + 1]], axis=1))
            o2 = dot(q2, th)
            out = o2[:96] + o2[96:] + dot(q2[:96], tl)
            for d in range(2):
                yg[s, 0, k + d] = out[:48, 128 * d:128 * d + 128]
                yg[s, 1, k + d] = out[48:, 128 * d:128 * d + 128]
        src = ((z + dz) % 4) * 2 + c
        cp = pltpu.make_async_remote_copy(
            src_ref=yg.at[s, 1 - c], dst_ref=o_ref.at[pl.ds(0, KG), pl.ds(0, 48), cols(src)],
            send_sem=xsem.at[s], recv_sem=wsem.at[s],
            device_id=(gx, z * 2 + 1 - c), device_id_type=pl.DeviceIdType.MESH)
        cp.start()
        sends.append(cp)
        cp = pltpu.make_async_copy(yg.at[s, c], o_ref.at[pl.ds(0, KG), pl.ds(0, 48), cols(src)], osem.at[s])
        cp.start()
        locs.append(cp)
    for cp in sends:
        cp.wait()
    for cp in locs:
        cp.wait()


def core_out(basis_t, tensor, below, above, far):
    f = jnp.float32
    V, D = pltpu.VMEM, pltpu.SemaphoreType.DMA
    ng = len(GROUPS)
    ANY = pl.BlockSpec(memory_space=pl.ANY)
    return pl.pallas_call(
        core_kernel,
        out_shape=jax.ShapeDtypeStruct((16, 48, 1024), f),
        in_specs=[pl.BlockSpec(memory_space=pltpu.VMEM)] + [ANY] * 4,
        out_specs=pl.BlockSpec(memory_space=pltpu.VMEM),
        scratch_shapes=[V((16 - KG, 512, 128), f), V((4, KG, 512, 128), f), V((384, 512), jnp.bfloat16), V((384, 512), jnp.bfloat16),
                        V((16 - KG, 384, 128), f), V((4, 2, KG, 48, 128), f),
                        D((ng,)), D((4,)), D((7, ng)), D((7, ng)), D((4,)), D((4,)), D((5,))],
        compiler_params=pltpu.CompilerParams(collective_id=1, has_side_effects=True, vmem_limit_bytes=24 << 20),
        name="core_out",
    )(basis_t, tensor, below, above, far)


def body(tensor, start_basis):
    packed, early = gram_sum(tensor)
    basis_t, below, above, far = sweeps(packed, start_basis, early)
    return core_out(basis_t, tensor, below, above, far)


def solution(mesh):
    placed = (P("gx", None, "gy"), P())
    return jax.shard_map(
        body, mesh=mesh, in_specs=placed, out_specs=P("gx", "gy", None), check_vma=False
    )
```

```python
import jax
import jax.numpy as jnp
from jax import lax
from jax.experimental import pallas as pl
from jax.experimental.pallas import tpu as pltpu
from jax.sharding import PartitionSpec as P
MESH = pl.DeviceIdType.MESH
BF = jnp.bfloat16
BLOCKS = [(i, j) for i in range(4) for j in range(i + 1)]
OFFS = sorted(((dx, dy) for dx in range(4) for dy in range(4)), key=lambda o: -(min(o[0], 4 - o[0]) + min(o[1], 4 - o[1])))
SELF = 15
NT = (((1,), (1,)), ((), ()))


def ar_kernel(t_ref, o_ref, hb, lb, gp, ra, aa, rb, ab, rc, ac, sa, qa, sb, qb, sc, qc, sd, qd, se, qe):
    gx = lax.axis_index("gx")
    gy = lax.axis_index("gy")
    x, y, z, c = gx // 4, gx % 4, gy // 2, gy % 2
    mate = z * 2 + 1 - c

    def plane(k, sign):
        dx, dy = OFFS[k]
        return ((x + sign * dx + 4) % 4) * 4 + (y + sign * dy + 4) % 4

    barrier = pltpu.get_barrier_semaphore()
    pl.semaphore_signal(barrier, inc=1, device_id=(gx, mate), device_id_type=MESH)
    for k in range(15):
        pl.semaphore_signal(barrier, inc=1, device_id=(plane(k, 1), gy), device_id_type=MESH)
    for d in range(1, 4):
        pl.semaphore_signal(barrier, inc=1, device_id=(gx, ((z + d) % 4) * 2 + c), device_id_type=MESH)

    for s in range(16):
        v = t_ref[s]
        h = v.astype(BF)
        hb[:, 128 * s:128 * s + 128] = h
        lb[:, 128 * s:128 * s + 128] = (v - h.astype(jnp.float32)).astype(BF)

    def dot(a, b):
        return lax.dot_general(a, b, NT, preferred_element_type=jnp.float32)

    for (r0, c0) in ((0, 0), (256, 0), (256, 256)):
        hr, lr = hb[r0:r0 + 256, :], lb[r0:r0 + 256, :]
        hc, lc = hb[c0:c0 + 256, :], lb[c0:c0 + 256, :]
        g = dot(hr, hc) + dot(hr, lc) + dot(lr, hc)
        for n, (i, j) in enumerate(BLOCKS):
            if r0 <= 128 * i < r0 + 256 and c0 <= 128 * j < c0 + 256:
                gp[16 * n:16 * n + 16] = g[128 * i - r0:128 * i - r0 + 128, 128 * j - c0:128 * j - c0 + 128].reshape(16, 8, 128)

    pl.semaphore_wait(barrier, 19)
    pieces = lambda core, g: pl.ds(80 * core + 5 * g, 5)

    def remote(src, dst, ss, rs, dev):
        return pltpu.make_async_remote_copy(src_ref=src, dst_ref=dst, send_sem=ss, recv_sem=rs, device_id=dev, device_id_type=MESH)

    A = [remote(gp.at[pieces(1 - c, plane(k, 1))], ra.at[k], sa.at[k], qa.at[k], (gx, mate)) for k in range(16)]
    for cp in A:
        cp.start()
    B = []
    for k in range(16):
        A[k].wait_recv()
        aa[k] = gp[pieces(c, plane(k, 1))] + ra[k]
        if k != SELF:
            cp = remote(aa.at[k], rb.at[k], sb.at[k], qb.at[k], (plane(k, 1), gy))
            cp.start()
            B.append(cp)
    total = aa[SELF]
    for k in range(14, -1, -1):
        B[k].wait_recv()
        total = total + rb[k]
    ab[...] = total
    rc[z] = total
    C = []
    for d in range(1, 4):
        cp = remote(ab, rc.at[z], sc.at[d], qc.at[d], (gx, ((z + d) % 4) * 2 + c))
        cp.start()
        C.append(cp)
    for cp in C:
        cp.wait_recv()
    total = (rc[0] + rc[1]) + (rc[2] + rc[3])
    ac[...] = total
    mine = pieces(c, gx)
    D = []
    for k in range(15):
        cp = remote(ac, o_ref.at[mine], sd.at[k], qd.at[k], (plane(k, 1), gy))
        cp.start()
        D.append(cp)
    o_ref[mine] = total
    E = [remote(ac, o_ref.at[mine], se.at[SELF], qe.at[SELF], (gx, mate))]
    E[0].start()
    for k in range(14, -1, -1):
        D[k].wait_recv()
        spot = pieces(c, plane(k, -1))
        cp = remote(o_ref.at[spot], o_ref.at[spot], se.at[k], qe.at[k], (gx, mate))
        cp.start()
        E.append(cp)
    for cp in E:
        cp.wait_recv()
    for cp in A + B + C + D + E:
        cp.wait_send()


def gram_sum(tensor):
    f = jnp.float32
    V, D = pltpu.VMEM, pltpu.SemaphoreType.DMA
    return pl.pallas_call(
        ar_kernel,
        out_shape=jax.ShapeDtypeStruct((160, 8, 128), f),
        in_specs=[pl.BlockSpec(memory_space=pltpu.VMEM)],
        out_specs=pl.BlockSpec(memory_space=pltpu.VMEM),
        scratch_shapes=[
            V((512, 2048), BF), V((512, 2048), BF),
            V((160, 8, 128), f), V((16, 5, 8, 128), f), V((16, 5, 8, 128), f), V((16, 5, 8, 128), f),
            V((5, 8, 128), f), V((4, 5, 8, 128), f), V((5, 8, 128), f),
            D((16,)), D((16,)), D((16,)), D((16,)), D((4,)), D((4,)), D((16,)), D((16,)), D((16,)), D((16,)),
        ],
        compiler_params=pltpu.CompilerParams(collective_id=0, has_side_effects=True, vmem_limit_bytes=28 << 20),
        name="gram_sum",
    )(tensor)


def split(x):
    h = x.astype(jnp.bfloat16)
    return h, (x - h.astype(jnp.float32)).astype(jnp.bfloat16)


def mm(a, b, ca=1, cb=0):
    ah, al = split(a)
    bh, bl = split(b)

    def dot(u, v):
        return lax.dot_general(u, v, (((ca,), (cb,)), ((), ())), preferred_element_type=jnp.float32)

    return dot(ah, bh) + (dot(ah, bl) + dot(al, bh))


LOOK = 2


def lanes(x, i):
    return jnp.broadcast_to(x[:, i:i + 1], (8, 128))


def rows(x, i):
    return jnp.broadcast_to(x[i:i + 1, :], (8, 128))


def chol_steps(A, one, li):
    row = lax.broadcasted_iota(jnp.int32, (8, 128), 0)
    lane = lax.broadcasted_iota(jnp.int32, (8, 128), 1)
    C = [lanes(A[0], j) * one for j in range(8)]
    for p in range(16):
        c = 8 * p
        done = (lane >= c) & (lane < c + 8)
        S = [[rows(C[j], i) for j in range(i + 1)] for i in range(8)]
        top = jnp.where(done, jnp.where(lane == row + c, 1.0, 0.0), A[p])
        V = [rows(top, i) for i in range(8)]
        near = range(p + 1, min(p + 1 + LOOK, 16))
        if p < 15:
            C = [lanes(A[p + 1], c + 8 + j) for j in range(8)]
        X = {g: [lanes(A[g], c + j) for j in range(8)] for g in range(p + 1, 16)}
        for g in range(p + 1, 16):
            A[g] = jnp.where(done, 0.0, A[g])
        L = [[None] * 8 for _ in range(8)]
        r = [None] * 8
        for j in range(8):
            r[j] = lax.rsqrt(S[j][j])
            for i in range(j + 1, 8):
                L[i][j] = S[i][j] * r[j]
            for i in range(j + 1, 8):
                for k in range(j + 1, i + 1):
                    S[i][k] = S[i][k] - L[i][j] * L[k][j]
            V[j] = V[j] * r[j]
            for g in near:
                x = X[g][j] * r[j]
                for k in range(j + 1, 8):
                    X[g][k] = X[g][k] - x * L[k][j]
                A[g] = A[g] - x * V[j]
                if g == p + 1:
                    for k in range(8):
                        C[k] = C[k] - x * rows(x, k)
            for i in range(j + 1, 8):
                V[i] = V[i] - L[i][j] * V[j]
        o = V[0]
        for i in range(1, 8):
            o = jnp.where(row == i, V[i], o)
        li[c:c + 8, :] = jnp.where(lane < c + 8, o, 0.0)
        yield
        if p + 1 + LOOK >= 16:
            continue
        F = list(V)
        for j in range(7, -1, -1):
            F[j] = F[j] * r[j]
            for i in range(j):
                F[i] = F[i] - L[j][i] * F[j]
        for g in range(p + 1 + LOOK, 16):
            t = [X[g][j] * F[j] for j in range(8)]
            t = [t[0] + t[1], t[2] + t[3], t[4] + t[5], t[6] + t[7]]
            A[g] = A[g] - ((t[0] + t[1]) + (t[2] + t[3]))


def groups(ref):
    return [ref[8 * g:8 * g + 8, :] for g in range(16)]


def run(*steps):
    steps = list(steps)
    while steps:
        for one in list(steps):
            if next(one, True) is True:
                steps.remove(one)


def sweeps_kernel(p_ref, b_ref, o_ref, g_ref, p, q, a, li, one_ref):
    n = 0
    for i in range(4):
        for j in range(i + 1):
            blk = p_ref[16 * n:16 * n + 16].reshape(128, 128)
            g_ref[128 * i:128 * i + 128, 128 * j:128 * j + 128] = blk
            if j < i:
                g_ref[128 * j:128 * j + 128, 128 * i:128 * i + 128] = blk.T
            n += 1
    one_ref[...] = jnp.ones((8, 128), jnp.float32)
    one = one_ref[...]
    first, second = 0, 3

    def product(s, k, source, cs):
        p[s + k] = mm(source, g_ref[...], cs, 0)
        for j in range(k + 1):
            a[s + j, k] = mm(p[s + j], p[s + k], 1, 1)

    def basis(s, k):
        q[s + k] = mm(li[s + k], p[s + k])

    def factor(s, k, j):
        a[s + k, j] = mm(li[s + k], a[s + k, j])

    def reduce_gram(s, k, i, j):
        a[s + i, j] -= mm(a[s + k, i], a[s + k, j], 0, 0)

    def reduce_product(s, k, j):
        p[s + j] -= mm(a[s + k, j], q[s + k], 0, 0)

    def chol(s, k):
        return chol_steps(groups(a.at[s + k, k]), one, li.at[s + k])

    for k in range(3):
        product(first, k, b_ref[:, 128 * k:128 * k + 128], 0)
    run(chol(first, 0))
    factor(first, 0, 1)
    reduce_gram(first, 0, 1, 1)
    basis(first, 0)
    product(second, 0, q[0], 1)
    factor(first, 0, 2)
    reduce_gram(first, 0, 1, 2)
    reduce_gram(first, 0, 2, 2)
    reduce_product(first, 0, 1)
    reduce_product(first, 0, 2)
    run(chol(first, 1), chol(second, 0))
    factor(first, 1, 2)
    reduce_gram(first, 1, 2, 2)
    basis(first, 1)
    product(second, 1, q[1], 1)
    factor(second, 0, 1)
    reduce_gram(second, 0, 1, 1)
    reduce_product(first, 1, 2)
    basis(second, 0)
    reduce_product(second, 0, 1)
    run(chol(first, 2), chol(second, 1))
    basis(first, 2)
    product(second, 2, q[2], 1)
    factor(second, 0, 2)
    reduce_gram(second, 0, 2, 2)
    factor(second, 1, 2)
    reduce_gram(second, 1, 2, 2)
    basis(second, 1)
    reduce_product(second, 0, 2)
    reduce_product(second, 1, 2)
    run(chol(second, 2))
    basis(second, 2)
    for k in range(3):
        o_ref[128 * k:128 * k + 128, :] = q[3 + k]


def sweeps(packed, start):
    f = jnp.float32
    whole = pl.BlockSpec(memory_space=pltpu.VMEM)
    return pl.pallas_call(
        sweeps_kernel,
        out_shape=jax.ShapeDtypeStruct((384, 512), f),
        in_specs=[whole] * 2, out_specs=whole,
        scratch_shapes=[pltpu.VMEM((512, 512), f), pltpu.VMEM((6, 128, 512), f), pltpu.VMEM((6, 128, 512), f),
                        pltpu.VMEM((6, 3, 128, 128), f), pltpu.VMEM((6, 128, 128), f), pltpu.VMEM((8, 128), f)],
        cost_estimate=pl.CostEstimate(flops=4000000000, bytes_accessed=3000000, transcendentals=0),
        compiler_params=pltpu.CompilerParams(vmem_limit_bytes=24 << 20), name="sweeps",
    )(packed, start)


RELS = [(2, 0), (2, 1), (1, 0), (3, 0), (1, 1), (3, 1), (0, 1)]
GROUPS = [(0, 2), (2, 4), (4, 8), (8, 12), (12, 16)]


def core_kernel(q_ref, t_ref, o_ref, qh, ql, y, ssem, rsem, osem):
    gx = lax.axis_index("gx")
    gy = lax.axis_index("gy")
    z, c = gy // 2, gy % 2

    def other(r):
        dz, dc = RELS[r]
        return ((z + dz) % 4) * 2 + (c + dc) % 2

    barrier = pltpu.get_barrier_semaphore()
    for r in range(7):
        pl.semaphore_signal(barrier, inc=1, device_id=(gx, other(r)), device_id_type=pl.DeviceIdType.MESH)
    v = q_ref[...]
    h = v.astype(jnp.bfloat16)
    qh[...] = h
    ql[...] = (v - h.astype(jnp.float32)).astype(jnp.bfloat16)

    def dot(a, b):
        return jnp.dot(a, b, preferred_element_type=jnp.float32)

    spot = pl.ds(pl.multiple_of(gy * 128, 128), 128)
    sends = []
    for n, (a, b) in enumerate(GROUPS):
        for k in range(a, b, 2):
            v = jnp.concatenate([t_ref[k], t_ref[k + 1]], axis=1)
            th = v.astype(jnp.bfloat16)
            tl = (v - th.astype(jnp.float32)).astype(jnp.bfloat16)
            out = dot(qh[...], th) + dot(qh[...], tl) + dot(ql[...], th)
            y[k] = out[:, :128]
            y[k + 1] = out[:, 128:]
        if n == 0:
            pl.semaphore_wait(barrier, 7)
        for r in range(7):
            cp = pltpu.make_async_remote_copy(
                src_ref=y.at[pl.ds(a, b - a), pl.ds(pl.multiple_of(48 * other(r), 8), 48)],
                dst_ref=o_ref.at[pl.ds(a, b - a), pl.ds(0, 48), spot],
                send_sem=ssem.at[r, n], recv_sem=rsem.at[r, n],
                device_id=(gx, other(r)), device_id_type=pl.DeviceIdType.MESH)
            cp.start()
            sends.append(cp)
    own = pltpu.make_async_copy(y.at[pl.ds(0, 16), pl.ds(pl.multiple_of(48 * gy, 8), 48)], o_ref.at[pl.ds(0, 16), pl.ds(0, 48), spot], osem)
    own.start()
    for cp in sends:
        cp.wait()
    own.wait()


def core_out(basis_t, tensor):
    f = jnp.float32
    V, D = pltpu.VMEM, pltpu.SemaphoreType.DMA
    ng = len(GROUPS)
    return pl.pallas_call(
        core_kernel,
        out_shape=jax.ShapeDtypeStruct((16, 48, 1024), f),
        in_specs=[pl.BlockSpec(memory_space=pltpu.VMEM), pl.BlockSpec(memory_space=pltpu.VMEM)],
        out_specs=pl.BlockSpec(memory_space=pltpu.VMEM),
        scratch_shapes=[V((384, 512), jnp.bfloat16), V((384, 512), jnp.bfloat16), V((16, 384, 128), f),
                        D((7, ng)), D((7, ng)), D],
        compiler_params=pltpu.CompilerParams(collective_id=1, has_side_effects=True, vmem_limit_bytes=20 << 20),
        name="core_out",
    )(basis_t, tensor)


def body(tensor, start_basis):
    return core_out(sweeps(gram_sum(tensor), start_basis), tensor)


def solution(mesh):
    placed = (P("gx", None, "gy"), P())
    return jax.shard_map(
        body, mesh=mesh, in_specs=placed, out_specs=P("gx", "gy", None), check_vma=False
    )
```

```python
import jax
import jax.numpy as jnp
from jax import lax
from jax.experimental import pallas as pl
from jax.experimental.pallas import tpu as pltpu
from jax.sharding import PartitionSpec as P
MESH = pl.DeviceIdType.MESH
BF = jnp.bfloat16
BLOCKS = [(i, j) for i in range(4) for j in range(i + 1)]
OFFS = sorted(((dx, dy) for dx in range(4) for dy in range(4)), key=lambda o: -(min(o[0], 4 - o[0]) + min(o[1], 4 - o[1])))
SELF = 15
NT = (((1,), (1,)), ((), ()))


def ar_kernel(t_ref, o_ref, hb, lb, gp, ra, aa, rb, ab, rc, ac, sa, qa, sb, qb, sc, qc, sd, qd, se, qe):
    gx = lax.axis_index("gx")
    gy = lax.axis_index("gy")
    x, y, z, c = gx // 4, gx % 4, gy // 2, gy % 2
    mate = z * 2 + 1 - c

    def plane(k, sign):
        dx, dy = OFFS[k]
        return ((x + sign * dx + 4) % 4) * 4 + (y + sign * dy + 4) % 4

    barrier = pltpu.get_barrier_semaphore()
    pl.semaphore_signal(barrier, inc=1, device_id=(gx, mate), device_id_type=MESH)
    for k in range(15):
        pl.semaphore_signal(barrier, inc=1, device_id=(plane(k, 1), gy), device_id_type=MESH)
    for d in range(1, 4):
        pl.semaphore_signal(barrier, inc=1, device_id=(gx, ((z + d) % 4) * 2 + c), device_id_type=MESH)

    for s in range(16):
        v = t_ref[s]
        h = v.astype(BF)
        hb[:, 128 * s:128 * s + 128] = h
        lb[:, 128 * s:128 * s + 128] = (v - h.astype(jnp.float32)).astype(BF)

    def dot(a, b):
        return lax.dot_general(a, b, NT, preferred_element_type=jnp.float32)

    for (r0, c0) in ((0, 0), (256, 0), (256, 256)):
        hr, lr = hb[r0:r0 + 256, :], lb[r0:r0 + 256, :]
        hc, lc = hb[c0:c0 + 256, :], lb[c0:c0 + 256, :]
        g = dot(hr, hc) + dot(hr, lc) + dot(lr, hc)
        for n, (i, j) in enumerate(BLOCKS):
            if r0 <= 128 * i < r0 + 256 and c0 <= 128 * j < c0 + 256:
                gp[16 * n:16 * n + 16] = g[128 * i - r0:128 * i - r0 + 128, 128 * j - c0:128 * j - c0 + 128].reshape(16, 8, 128)

    pl.semaphore_wait(barrier, 19)
    pieces = lambda core, g: pl.ds(80 * core + 5 * g, 5)

    def remote(src, dst, ss, rs, dev):
        return pltpu.make_async_remote_copy(src_ref=src, dst_ref=dst, send_sem=ss, recv_sem=rs, device_id=dev, device_id_type=MESH)

    A = [remote(gp.at[pieces(1 - c, plane(k, 1))], ra.at[k], sa.at[k], qa.at[k], (gx, mate)) for k in range(16)]
    for cp in A:
        cp.start()
    B = []
    for k in range(16):
        A[k].wait_recv()
        aa[k] = gp[pieces(c, plane(k, 1))] + ra[k]
        if k != SELF:
            cp = remote(aa.at[k], rb.at[k], sb.at[k], qb.at[k], (plane(k, 1), gy))
            cp.start()
            B.append(cp)
    total = aa[SELF]
    for k in range(14, -1, -1):
        B[k].wait_recv()
        total = total + rb[k]
    ab[...] = total
    rc[z] = total
    C = []
    for d in range(1, 4):
        cp = remote(ab, rc.at[z], sc.at[d], qc.at[d], (gx, ((z + d) % 4) * 2 + c))
        cp.start()
        C.append(cp)
    for cp in C:
        cp.wait_recv()
    total = (rc[0] + rc[1]) + (rc[2] + rc[3])
    ac[...] = total
    mine = pieces(c, gx)
    D = []
    for k in range(15):
        cp = remote(ac, o_ref.at[mine], sd.at[k], qd.at[k], (plane(k, 1), gy))
        cp.start()
        D.append(cp)
    o_ref[mine] = total
    E = [remote(ac, o_ref.at[mine], se.at[SELF], qe.at[SELF], (gx, mate))]
    E[0].start()
    for k in range(14, -1, -1):
        D[k].wait_recv()
        spot = pieces(c, plane(k, -1))
        cp = remote(o_ref.at[spot], o_ref.at[spot], se.at[k], qe.at[k], (gx, mate))
        cp.start()
        E.append(cp)
    for cp in E:
        cp.wait_recv()
    for cp in A + B + C + D + E:
        cp.wait_send()


def gram_sum(tensor):
    f = jnp.float32
    V, D = pltpu.VMEM, pltpu.SemaphoreType.DMA
    return pl.pallas_call(
        ar_kernel,
        out_shape=jax.ShapeDtypeStruct((160, 8, 128), f),
        in_specs=[pl.BlockSpec(memory_space=pltpu.VMEM)],
        out_specs=pl.BlockSpec(memory_space=pltpu.VMEM),
        scratch_shapes=[
            V((512, 2048), BF), V((512, 2048), BF),
            V((160, 8, 128), f), V((16, 5, 8, 128), f), V((16, 5, 8, 128), f), V((16, 5, 8, 128), f),
            V((5, 8, 128), f), V((4, 5, 8, 128), f), V((5, 8, 128), f),
            D((16,)), D((16,)), D((16,)), D((16,)), D((4,)), D((4,)), D((16,)), D((16,)), D((16,)), D((16,)),
        ],
        compiler_params=pltpu.CompilerParams(collective_id=0, has_side_effects=True, vmem_limit_bytes=16 << 20),
        name="gram_sum",
    )(tensor)


KG = 2


def split(x):
    h = x.astype(jnp.bfloat16)
    return h, (x - h.astype(jnp.float32)).astype(jnp.bfloat16)


def mm(a, b, ca=1, cb=0):
    ah, al = split(a)
    bh, bl = split(b)

    def dot(u, v):
        return lax.dot_general(u, v, (((ca,), (cb,)), ((), ())), preferred_element_type=jnp.float32)

    return dot(ah, bh) + (dot(ah, bl) + dot(al, bh))


LOOK = 2


def lanes(x, i):
    return jnp.broadcast_to(x[:, i:i + 1], (8, 128))


def rows(x, i):
    return jnp.broadcast_to(x[i:i + 1, :], (8, 128))


def chol_steps(A, one, li):
    row = lax.broadcasted_iota(jnp.int32, (8, 128), 0)
    lane = lax.broadcasted_iota(jnp.int32, (8, 128), 1)
    C = [lanes(A[0], j) * one for j in range(8)]
    for p in range(16):
        c = 8 * p
        done = (lane >= c) & (lane < c + 8)
        S = [[rows(C[j], i) for j in range(i + 1)] for i in range(8)]
        top = jnp.where(done, jnp.where(lane == row + c, 1.0, 0.0), A[p])
        V = [rows(top, i) for i in range(8)]
        near = range(p + 1, min(p + 1 + LOOK, 16))
        if p < 15:
            C = [lanes(A[p + 1], c + 8 + j) for j in range(8)]
        X = {g: [lanes(A[g], c + j) for j in range(8)] for g in range(p + 1, 16)}
        for g in range(p + 1, 16):
            A[g] = jnp.where(done, 0.0, A[g])
        L = [[None] * 8 for _ in range(8)]
        r = [None] * 8
        for j in range(8):
            r[j] = lax.rsqrt(S[j][j])
            for i in range(j + 1, 8):
                L[i][j] = S[i][j] * r[j]
            for i in range(j + 1, 8):
                for k in range(j + 1, i + 1):
                    S[i][k] = S[i][k] - L[i][j] * L[k][j]
            V[j] = V[j] * r[j]
            for g in near:
                x = X[g][j] * r[j]
                for k in range(j + 1, 8):
                    X[g][k] = X[g][k] - x * L[k][j]
                A[g] = A[g] - x * V[j]
                if g == p + 1:
                    for k in range(8):
                        C[k] = C[k] - x * rows(x, k)
            for i in range(j + 1, 8):
                V[i] = V[i] - L[i][j] * V[j]
        o = V[0]
        for i in range(1, 8):
            o = jnp.where(row == i, V[i], o)
        li[c:c + 8, :] = jnp.where(lane < c + 8, o, 0.0)
        yield
        if p + 1 + LOOK >= 16:
            continue
        F = list(V)
        for j in range(7, -1, -1):
            F[j] = F[j] * r[j]
            for i in range(j):
                F[i] = F[i] - L[j][i] * F[j]
        for g in range(p + 1 + LOOK, 16):
            t = [X[g][j] * F[j] for j in range(8)]
            t = [t[0] + t[1], t[2] + t[3], t[4] + t[5], t[6] + t[7]]
            A[g] = A[g] - ((t[0] + t[1]) + (t[2] + t[3]))


def groups(ref):
    return [ref[8 * g:8 * g + 8, :] for g in range(16)]


def run(*steps):
    steps = list(steps)
    while steps:
        for one in list(steps):
            if next(one, True) is True:
                steps.remove(one)


def sweeps_kernel(p_ref, b_ref, t_ref, o_ref, below, above, g_ref, p, q, a, li, one_ref, ssem, rsem):
    gx = lax.axis_index("gx")
    gy = lax.axis_index("gy")
    up, down = (gy + 2) % 8, (gy + 6) % 8
    barrier = pltpu.get_barrier_semaphore()
    for dev in (up, down):
        pl.semaphore_signal(barrier, inc=1, device_id=(gx, dev), device_id_type=pl.DeviceIdType.MESH)
    moves = []

    def move(src, dst, dev):
        n = len(moves)
        cp = pltpu.make_async_remote_copy(src_ref=src, dst_ref=dst, send_sem=ssem.at[n], recv_sem=rsem.at[n], device_id=(gx, dev), device_id_type=pl.DeviceIdType.MESH)
        cp.start()
        moves.append(cp)

    n = 0
    for i in range(4):
        for j in range(i + 1):
            blk = p_ref[16 * n:16 * n + 16].reshape(128, 128)
            g_ref[128 * i:128 * i + 128, 128 * j:128 * j + 128] = blk
            if j < i:
                g_ref[128 * j:128 * j + 128, 128 * i:128 * i + 128] = blk.T
            n += 1
    pl.semaphore_wait(barrier, 2)
    for n in range(KG):
        move(t_ref.at[n], below.at[n], up)
        move(t_ref.at[n], above.at[n], down)
    one_ref[...] = jnp.ones((8, 128), jnp.float32)
    one = one_ref[...]
    first, second = 0, 3

    def product(s, k, source, cs):
        p[s + k] = mm(source, g_ref[...], cs, 0)
        for j in range(k + 1):
            a[s + j, k] = mm(p[s + j], p[s + k], 1, 1)

    def basis(s, k):
        q[s + k] = mm(li[s + k], p[s + k])

    def factor(s, k, j):
        a[s + k, j] = mm(li[s + k], a[s + k, j])

    def reduce_gram(s, k, i, j):
        a[s + i, j] -= mm(a[s + k, i], a[s + k, j], 0, 0)

    def reduce_product(s, k, j):
        p[s + j] -= mm(a[s + k, j], q[s + k], 0, 0)

    def chol(s, k):
        return chol_steps(groups(a.at[s + k, k]), one, li.at[s + k])

    for k in range(3):
        product(first, k, b_ref[:, 128 * k:128 * k + 128], 0)
    run(chol(first, 0))
    factor(first, 0, 1)
    reduce_gram(first, 0, 1, 1)
    basis(first, 0)
    product(second, 0, q[0], 1)
    factor(first, 0, 2)
    reduce_gram(first, 0, 1, 2)
    reduce_gram(first, 0, 2, 2)
    reduce_product(first, 0, 1)
    reduce_product(first, 0, 2)
    run(chol(first, 1), chol(second, 0))
    factor(first, 1, 2)
    reduce_gram(first, 1, 2, 2)
    basis(first, 1)
    product(second, 1, q[1], 1)
    factor(second, 0, 1)
    reduce_gram(second, 0, 1, 1)
    reduce_product(first, 1, 2)
    basis(second, 0)
    reduce_product(second, 0, 1)
    run(chol(first, 2), chol(second, 1))
    basis(first, 2)
    product(second, 2, q[2], 1)
    factor(second, 0, 2)
    reduce_gram(second, 0, 2, 2)
    factor(second, 1, 2)
    reduce_gram(second, 1, 2, 2)
    basis(second, 1)
    reduce_product(second, 0, 2)
    reduce_product(second, 1, 2)
    run(chol(second, 2))
    basis(second, 2)
    for k in range(3):
        o_ref[128 * k:128 * k + 128, :] = q[3 + k]
    for cp in moves:
        cp.wait()


def sweeps(packed, start, tensor):
    f = jnp.float32
    whole = pl.BlockSpec(memory_space=pltpu.VMEM)
    anywhere = pl.BlockSpec(memory_space=pl.ANY)
    return pl.pallas_call(
        sweeps_kernel,
        out_shape=(jax.ShapeDtypeStruct((384, 512), f),) + (jax.ShapeDtypeStruct((KG, 512, 128), f),) * 2,
        in_specs=[whole] * 2 + [anywhere], out_specs=(whole,) + (anywhere,) * 2,
        scratch_shapes=[pltpu.VMEM((512, 512), f), pltpu.VMEM((6, 128, 512), f), pltpu.VMEM((6, 128, 512), f),
                        pltpu.VMEM((6, 3, 128, 128), f), pltpu.VMEM((6, 128, 128), f), pltpu.VMEM((8, 128), f),
                        pltpu.SemaphoreType.DMA((2 * KG,)), pltpu.SemaphoreType.DMA((2 * KG,))],
        cost_estimate=pl.CostEstimate(flops=4000000000, bytes_accessed=3000000, transcendentals=0),
        compiler_params=pltpu.CompilerParams(collective_id=2, has_side_effects=True, vmem_limit_bytes=12 << 20), name="sweeps",
    )(packed, start, tensor)


RELS = [(2, 0), (2, 1), (1, 0), (3, 0), (1, 1), (3, 1), (0, 1)]
GROUPS = [(2, 4), (4, 6), (6, 10), (10, 16), (0, KG)]


def core_kernel(q_ref, t_ref, below, above, o_ref, qh, ql, y, yg, ssem, rsem, xsem, wsem, osem):
    gx = lax.axis_index("gx")
    gy = lax.axis_index("gy")
    z, c = gy // 2, gy % 2

    def other(r):
        dz, dc = RELS[r]
        return ((z + dz) % 4) * 2 + (c + dc) % 2

    barrier = pltpu.get_barrier_semaphore()
    for r in range(7):
        pl.semaphore_signal(barrier, inc=1, device_id=(gx, other(r)), device_id_type=pl.DeviceIdType.MESH)
    v = q_ref[...]
    h = v.astype(jnp.bfloat16)
    qh[...] = h
    ql[...] = (v - h.astype(jnp.float32)).astype(jnp.bfloat16)

    def dot(a, b):
        return jnp.dot(a, b, preferred_element_type=jnp.float32)

    spot = pl.ds(pl.multiple_of(gy * 128, 128), 128)
    sends = []
    for n, (a, b) in enumerate(GROUPS):
        for k in range(a, b, 2):
            v = jnp.concatenate([t_ref[k], t_ref[k + 1]], axis=1)
            th = v.astype(jnp.bfloat16)
            tl = (v - th.astype(jnp.float32)).astype(jnp.bfloat16)
            out = dot(qh[...], th) + dot(qh[...], tl) + dot(ql[...], th)
            y[k] = out[:, :128]
            y[k + 1] = out[:, 128:]
        if n == 0:
            pl.semaphore_wait(barrier, 7)
        for r in range(7):
            if b <= KG and RELS[r][0] % 2 == 1:
                continue
            cp = pltpu.make_async_remote_copy(
                src_ref=y.at[pl.ds(a, b - a), pl.ds(pl.multiple_of(48 * other(r), 8), 48)],
                dst_ref=o_ref.at[pl.ds(a, b - a), pl.ds(0, 48), spot],
                send_sem=ssem.at[r, n], recv_sem=rsem.at[r, n],
                device_id=(gx, other(r)), device_id_type=pl.DeviceIdType.MESH)
            cp.start()
            sends.append(cp)
    own = pltpu.make_async_copy(y.at[pl.ds(0, 16), pl.ds(pl.multiple_of(48 * gy, 8), 48)], o_ref.at[pl.ds(0, 16), pl.ds(0, 48), spot], osem.at[2])
    own.start()
    rows = pl.ds(pl.multiple_of(96 * z, 32), 96)
    q2 = jnp.concatenate([qh[rows, :], ql[rows, :]], axis=0)
    locs = [own]
    for s, (got, dz) in enumerate(((below, 3), (above, 1))):
        for k in range(0, KG, 2):
            v = jnp.concatenate([got[k], got[k + 1]], axis=1)
            th = v.astype(jnp.bfloat16)
            tl = (v - th.astype(jnp.float32)).astype(jnp.bfloat16)
            o2 = dot(q2, th)
            out = o2[:96] + o2[96:] + dot(q2[:96], tl)
            for d in range(2):
                yg[s, 0, k + d] = out[:48, 128 * d:128 * d + 128]
                yg[s, 1, k + d] = out[48:, 128 * d:128 * d + 128]
        src = ((z + dz) % 4) * 2 + c
        there = pl.ds(pl.multiple_of(src * 128, 128), 128)
        cp = pltpu.make_async_remote_copy(
            src_ref=yg.at[s, 1 - c], dst_ref=o_ref.at[pl.ds(0, KG), pl.ds(0, 48), there],
            send_sem=xsem.at[s], recv_sem=wsem.at[s],
            device_id=(gx, z * 2 + 1 - c), device_id_type=pl.DeviceIdType.MESH)
        cp.start()
        sends.append(cp)
        cp = pltpu.make_async_copy(yg.at[s, c], o_ref.at[pl.ds(0, KG), pl.ds(0, 48), there], osem.at[s])
        cp.start()
        locs.append(cp)
    for cp in sends:
        cp.wait()
    for cp in locs:
        cp.wait()


def core_out(basis_t, tensor, below, above):
    f = jnp.float32
    V, D = pltpu.VMEM, pltpu.SemaphoreType.DMA
    ng = len(GROUPS)
    return pl.pallas_call(
        core_kernel,
        out_shape=jax.ShapeDtypeStruct((16, 48, 1024), f),
        in_specs=[pl.BlockSpec(memory_space=pltpu.VMEM)] * 4,
        out_specs=pl.BlockSpec(memory_space=pltpu.VMEM),
        scratch_shapes=[V((384, 512), jnp.bfloat16), V((384, 512), jnp.bfloat16), V((16, 384, 128), f), V((2, 2, KG, 48, 128), f),
                        D((7, ng)), D((7, ng)), D((2,)), D((2,)), D((3,))],
        compiler_params=pltpu.CompilerParams(collective_id=1, has_side_effects=True, vmem_limit_bytes=20 << 20),
        name="core_out",
    )(basis_t, tensor, below, above)


def body(tensor, start_basis):
    basis_t, below, above = sweeps(gram_sum(tensor), start_basis, tensor)
    return core_out(basis_t, tensor, below, above)


def solution(mesh):
    placed = (P("gx", None, "gy"), P())
    return jax.shard_map(
        body, mesh=mesh, in_specs=placed, out_specs=P("gx", "gy", None), check_vma=False
    )
```

```python
import jax
import jax.numpy as jnp
from jax import lax
from jax.experimental import pallas as pl
from jax.experimental.pallas import tpu as pltpu
from jax.sharding import PartitionSpec as P
MESH = pl.DeviceIdType.MESH
BF = jnp.bfloat16
BLOCKS = [(i, j) for i in range(4) for j in range(i + 1)]
OFFS = sorted(((dx, dy) for dx in range(4) for dy in range(4)), key=lambda o: -(min(o[0], 4 - o[0]) + min(o[1], 4 - o[1])))
SELF = 15
NT = (((1,), (1,)), ((), ()))


def ar_kernel(t_ref, o_ref, hb, lb, gp, ra, aa, rb, ab, rc, ac, sa, qa, sb, qb, sc, qc, sd, qd, se, qe):
    gx = lax.axis_index("gx")
    gy = lax.axis_index("gy")
    x, y, z, c = gx // 4, gx % 4, gy // 2, gy % 2
    mate = z * 2 + 1 - c

    def plane(k, sign):
        dx, dy = OFFS[k]
        return ((x + sign * dx + 4) % 4) * 4 + (y + sign * dy + 4) % 4

    barrier = pltpu.get_barrier_semaphore()
    pl.semaphore_signal(barrier, inc=1, device_id=(gx, mate), device_id_type=MESH)
    for k in range(15):
        pl.semaphore_signal(barrier, inc=1, device_id=(plane(k, 1), gy), device_id_type=MESH)
    for d in range(1, 4):
        pl.semaphore_signal(barrier, inc=1, device_id=(gx, ((z + d) % 4) * 2 + c), device_id_type=MESH)

    for s in range(16):
        v = t_ref[s]
        h = v.astype(BF)
        hb[:, 128 * s:128 * s + 128] = h
        lb[:, 128 * s:128 * s + 128] = (v - h.astype(jnp.float32)).astype(BF)

    def dot(a, b):
        return lax.dot_general(a, b, NT, preferred_element_type=jnp.float32)

    for (r0, c0) in ((0, 0), (256, 0), (256, 256)):
        hr, lr = hb[r0:r0 + 256, :], lb[r0:r0 + 256, :]
        hc, lc = hb[c0:c0 + 256, :], lb[c0:c0 + 256, :]
        g = dot(hr, hc) + dot(hr, lc) + dot(lr, hc)
        for n, (i, j) in enumerate(BLOCKS):
            if r0 <= 128 * i < r0 + 256 and c0 <= 128 * j < c0 + 256:
                gp[16 * n:16 * n + 16] = g[128 * i - r0:128 * i - r0 + 128, 128 * j - c0:128 * j - c0 + 128].reshape(16, 8, 128)

    pl.semaphore_wait(barrier, 19)
    pieces = lambda core, g: pl.ds(80 * core + 5 * g, 5)

    def remote(src, dst, ss, rs, dev):
        return pltpu.make_async_remote_copy(src_ref=src, dst_ref=dst, send_sem=ss, recv_sem=rs, device_id=dev, device_id_type=MESH)

    A = [remote(gp.at[pieces(1 - c, plane(k, 1))], ra.at[k], sa.at[k], qa.at[k], (gx, mate)) for k in range(16)]
    for cp in A:
        cp.start()
    B = []
    for k in range(16):
        A[k].wait_recv()
        aa[k] = gp[pieces(c, plane(k, 1))] + ra[k]
        if k != SELF:
            cp = remote(aa.at[k], rb.at[k], sb.at[k], qb.at[k], (plane(k, 1), gy))
            cp.start()
            B.append(cp)
    total = aa[SELF]
    for k in range(14, -1, -1):
        B[k].wait_recv()
        total = total + rb[k]
    ab[...] = total
    rc[z] = total
    C = []
    for d in range(1, 4):
        cp = remote(ab, rc.at[z], sc.at[d], qc.at[d], (gx, ((z + d) % 4) * 2 + c))
        cp.start()
        C.append(cp)
    for cp in C:
        cp.wait_recv()
    total = (rc[0] + rc[1]) + (rc[2] + rc[3])
    ac[...] = total
    mine = pieces(c, gx)
    D = []
    for k in range(15):
        cp = remote(ac, o_ref.at[mine], sd.at[k], qd.at[k], (plane(k, 1), gy))
        cp.start()
        D.append(cp)
    o_ref[mine] = total
    E = [remote(ac, o_ref.at[mine], se.at[SELF], qe.at[SELF], (gx, mate))]
    E[0].start()
    for k in range(14, -1, -1):
        D[k].wait_recv()
        spot = pieces(c, plane(k, -1))
        cp = remote(o_ref.at[spot], o_ref.at[spot], se.at[k], qe.at[k], (gx, mate))
        cp.start()
        E.append(cp)
    for cp in E:
        cp.wait_recv()
    for cp in A + B + C + D + E:
        cp.wait_send()


def gram_sum(tensor):
    f = jnp.float32
    V, D = pltpu.VMEM, pltpu.SemaphoreType.DMA
    return pl.pallas_call(
        ar_kernel,
        out_shape=jax.ShapeDtypeStruct((160, 8, 128), f),
        in_specs=[pl.BlockSpec(memory_space=pltpu.VMEM)],
        out_specs=pl.BlockSpec(memory_space=pltpu.VMEM),
        scratch_shapes=[
            V((512, 2048), BF), V((512, 2048), BF),
            V((160, 8, 128), f), V((16, 5, 8, 128), f), V((16, 5, 8, 128), f), V((16, 5, 8, 128), f),
            V((5, 8, 128), f), V((4, 5, 8, 128), f), V((5, 8, 128), f),
            D((16,)), D((16,)), D((16,)), D((16,)), D((4,)), D((4,)), D((16,)), D((16,)), D((16,)), D((16,)),
        ],
        compiler_params=pltpu.CompilerParams(collective_id=0, has_side_effects=True, vmem_limit_bytes=28 << 20),
        name="gram_sum",
    )(tensor)


def split(x):
    h = x.astype(jnp.bfloat16)
    return h, (x - h.astype(jnp.float32)).astype(jnp.bfloat16)


def mm(a, b, ca=1, cb=0):
    ah, al = split(a)
    bh, bl = split(b)

    def dot(u, v):
        return lax.dot_general(u, v, (((ca,), (cb,)), ((), ())), preferred_element_type=jnp.float32)

    return dot(ah, bh) + (dot(ah, bl) + dot(al, bh))


LOOK = 2


def lanes(x, i):
    return jnp.broadcast_to(x[:, i:i + 1], (8, 128))


def rows(x, i):
    return jnp.broadcast_to(x[i:i + 1, :], (8, 128))


def chol_steps(A, one, li):
    row = lax.broadcasted_iota(jnp.int32, (8, 128), 0)
    lane = lax.broadcasted_iota(jnp.int32, (8, 128), 1)
    C = [lanes(A[0], j) * one for j in range(8)]
    for p in range(16):
        c = 8 * p
        done = (lane >= c) & (lane < c + 8)
        S = [[rows(C[j], i) for j in range(i + 1)] for i in range(8)]
        top = jnp.where(done, jnp.where(lane == row + c, 1.0, 0.0), A[p])
        V = [rows(top, i) for i in range(8)]
        near = range(p + 1, min(p + 1 + LOOK, 16))
        if p < 15:
            C = [lanes(A[p + 1], c + 8 + j) for j in range(8)]
        X = {g: [lanes(A[g], c + j) for j in range(8)] for g in range(p + 1, 16)}
        for g in range(p + 1, 16):
            A[g] = jnp.where(done, 0.0, A[g])
        L = [[None] * 8 for _ in range(8)]
        r = [None] * 8
        for j in range(8):
            r[j] = lax.rsqrt(S[j][j])
            for i in range(j + 1, 8):
                L[i][j] = S[i][j] * r[j]
            for i in range(j + 1, 8):
                for k in range(j + 1, i + 1):
                    S[i][k] = S[i][k] - L[i][j] * L[k][j]
            V[j] = V[j] * r[j]
            for g in near:
                x = X[g][j] * r[j]
                for k in range(j + 1, 8):
                    X[g][k] = X[g][k] - x * L[k][j]
                A[g] = A[g] - x * V[j]
                if g == p + 1:
                    for k in range(8):
                        C[k] = C[k] - x * rows(x, k)
            for i in range(j + 1, 8):
                V[i] = V[i] - L[i][j] * V[j]
        o = V[0]
        for i in range(1, 8):
            o = jnp.where(row == i, V[i], o)
        li[c:c + 8, :] = jnp.where(lane < c + 8, o, 0.0)
        yield
        if p + 1 + LOOK >= 16:
            continue
        F = list(V)
        for j in range(7, -1, -1):
            F[j] = F[j] * r[j]
            for i in range(j):
                F[i] = F[i] - L[j][i] * F[j]
        for g in range(p + 1 + LOOK, 16):
            t = [X[g][j] * F[j] for j in range(8)]
            t = [t[0] + t[1], t[2] + t[3], t[4] + t[5], t[6] + t[7]]
            A[g] = A[g] - ((t[0] + t[1]) + (t[2] + t[3]))


def groups(ref):
    return [ref[8 * g:8 * g + 8, :] for g in range(16)]


def run(*steps):
    steps = list(steps)
    while steps:
        for one in list(steps):
            if next(one, True) is True:
                steps.remove(one)


def sweeps_kernel(p_ref, b_ref, o_ref, g_ref, p, q, a, li, one_ref):
    n = 0
    for i in range(4):
        for j in range(i + 1):
            blk = p_ref[16 * n:16 * n + 16].reshape(128, 128)
            g_ref[128 * i:128 * i + 128, 128 * j:128 * j + 128] = blk
            if j < i:
                g_ref[128 * j:128 * j + 128, 128 * i:128 * i + 128] = blk.T
            n += 1
    one_ref[...] = jnp.ones((8, 128), jnp.float32)
    one = one_ref[...]
    first, second = 0, 3

    def product(s, k, source, cs):
        p[s + k] = mm(source, g_ref[...], cs, 0)
        for j in range(k + 1):
            a[s + j, k] = mm(p[s + j], p[s + k], 1, 1)

    def basis(s, k):
        q[s + k] = mm(li[s + k], p[s + k])

    def factor(s, k, j):
        a[s + k, j] = mm(li[s + k], a[s + k, j])

    def reduce_gram(s, k, i, j):
        a[s + i, j] -= mm(a[s + k, i], a[s + k, j], 0, 0)

    def reduce_product(s, k, j):
        p[s + j] -= mm(a[s + k, j], q[s + k], 0, 0)

    def chol(s, k):
        return chol_steps(groups(a.at[s + k, k]), one, li.at[s + k])

    for k in range(3):
        product(first, k, b_ref[:, 128 * k:128 * k + 128], 0)
    run(chol(first, 0))
    factor(first, 0, 1)
    reduce_gram(first, 0, 1, 1)
    basis(first, 0)
    product(second, 0, q[0], 1)
    factor(first, 0, 2)
    reduce_gram(first, 0, 1, 2)
    reduce_gram(first, 0, 2, 2)
    reduce_product(first, 0, 1)
    reduce_product(first, 0, 2)
    run(chol(first, 1), chol(second, 0))
    factor(first, 1, 2)
    reduce_gram(first, 1, 2, 2)
    basis(first, 1)
    product(second, 1, q[1], 1)
    factor(second, 0, 1)
    reduce_gram(second, 0, 1, 1)
    reduce_product(first, 1, 2)
    basis(second, 0)
    reduce_product(second, 0, 1)
    run(chol(first, 2), chol(second, 1))
    basis(first, 2)
    product(second, 2, q[2], 1)
    factor(second, 0, 2)
    reduce_gram(second, 0, 2, 2)
    factor(second, 1, 2)
    reduce_gram(second, 1, 2, 2)
    basis(second, 1)
    reduce_product(second, 0, 2)
    reduce_product(second, 1, 2)
    run(chol(second, 2))
    basis(second, 2)
    for k in range(3):
        o_ref[128 * k:128 * k + 128, :] = q[3 + k]


def sweeps(packed, start):
    f = jnp.float32
    whole = pl.BlockSpec(memory_space=pltpu.VMEM)
    return pl.pallas_call(
        sweeps_kernel,
        out_shape=jax.ShapeDtypeStruct((384, 512), f),
        in_specs=[whole] * 2, out_specs=whole,
        scratch_shapes=[pltpu.VMEM((512, 512), f), pltpu.VMEM((6, 128, 512), f), pltpu.VMEM((6, 128, 512), f),
                        pltpu.VMEM((6, 3, 128, 128), f), pltpu.VMEM((6, 128, 128), f), pltpu.VMEM((8, 128), f)],
        cost_estimate=pl.CostEstimate(flops=4000000000, bytes_accessed=3000000, transcendentals=0),
        compiler_params=pltpu.CompilerParams(vmem_limit_bytes=24 << 20), name="sweeps",
    )(packed, start)


RELS = [(2, 0), (2, 1), (1, 0), (3, 0), (1, 1), (3, 1), (0, 1)]
GROUPS = [(0, 2), (2, 6), (6, 16)]


def core_kernel(q_ref, t_ref, o_ref, qh, ql, y, ssem, rsem, osem):
    gx = lax.axis_index("gx")
    gy = lax.axis_index("gy")
    z, c = gy // 2, gy % 2

    def other(r):
        dz, dc = RELS[r]
        return ((z + dz) % 4) * 2 + (c + dc) % 2

    barrier = pltpu.get_barrier_semaphore()
    for r in range(7):
        pl.semaphore_signal(barrier, inc=1, device_id=(gx, other(r)), device_id_type=pl.DeviceIdType.MESH)
    v = q_ref[...]
    h = v.astype(jnp.bfloat16)
    qh[...] = h
    ql[...] = (v - h.astype(jnp.float32)).astype(jnp.bfloat16)

    def dot(a, b):
        return jnp.dot(a, b, preferred_element_type=jnp.float32)

    spot = pl.ds(pl.multiple_of(gy * 128, 128), 128)
    sends = []
    for n, (a, b) in enumerate(GROUPS):
        for k in range(a, b, 2):
            v = jnp.concatenate([t_ref[k], t_ref[k + 1]], axis=1)
            th = v.astype(jnp.bfloat16)
            tl = (v - th.astype(jnp.float32)).astype(jnp.bfloat16)
            out = dot(qh[...], th) + dot(qh[...], tl) + dot(ql[...], th)
            y[k] = out[:, :128]
            y[k + 1] = out[:, 128:]
        if n == 0:
            pl.semaphore_wait(barrier, 7)
        for r in range(7):
            cp = pltpu.make_async_remote_copy(
                src_ref=y.at[pl.ds(a, b - a), pl.ds(pl.multiple_of(48 * other(r), 8), 48)],
                dst_ref=o_ref.at[pl.ds(a, b - a), pl.ds(0, 48), spot],
                send_sem=ssem.at[r, n], recv_sem=rsem.at[r, n],
                device_id=(gx, other(r)), device_id_type=pl.DeviceIdType.MESH)
            cp.start()
            sends.append(cp)
    own = pltpu.make_async_copy(y.at[pl.ds(0, 16), pl.ds(pl.multiple_of(48 * gy, 8), 48)], o_ref.at[pl.ds(0, 16), pl.ds(0, 48), spot], osem)
    own.start()
    for cp in sends:
        cp.wait()
    own.wait()


def core_out(basis_t, tensor):
    f = jnp.float32
    V, D = pltpu.VMEM, pltpu.SemaphoreType.DMA
    ng = len(GROUPS)
    return pl.pallas_call(
        core_kernel,
        out_shape=jax.ShapeDtypeStruct((16, 48, 1024), f),
        in_specs=[pl.BlockSpec(memory_space=pltpu.VMEM), pl.BlockSpec(memory_space=pltpu.VMEM)],
        out_specs=pl.BlockSpec(memory_space=pltpu.VMEM),
        scratch_shapes=[V((384, 512), jnp.bfloat16), V((384, 512), jnp.bfloat16), V((16, 384, 128), f),
                        D((7, ng)), D((7, ng)), D],
        compiler_params=pltpu.CompilerParams(collective_id=1, has_side_effects=True, vmem_limit_bytes=20 << 20),
        name="core_out",
    )(basis_t, tensor)


def body(tensor, start_basis):
    return core_out(sweeps(gram_sum(tensor), start_basis), tensor)


def solution(mesh):
    placed = (P("gx", None, "gy"), P())
    return jax.shard_map(
        body, mesh=mesh, in_specs=placed, out_specs=P("gx", "gy", None), check_vma=False
    )
```

```python
import jax
import jax.numpy as jnp
from jax import lax
from jax.experimental import pallas as pl
from jax.experimental.pallas import tpu as pltpu
from jax.sharding import PartitionSpec as P
MESH = pl.DeviceIdType.MESH
BF = jnp.bfloat16
BLOCKS = [(i, j) for i in range(4) for j in range(i + 1)]
OFFS = sorted(((dx, dy) for dx in range(4) for dy in range(4)), key=lambda o: -(min(o[0], 4 - o[0]) + min(o[1], 4 - o[1])))
SELF = 15
NT = (((1,), (1,)), ((), ()))


def ar_kernel(t_ref, o_ref, hb, lb, gp, ra, aa, rb, ab, rc, ac, sa, qa, sb, qb, sc, qc, sd, qd, se, qe):
    gx = lax.axis_index("gx")
    gy = lax.axis_index("gy")
    x, y, z, c = gx // 4, gx % 4, gy // 2, gy % 2
    mate = z * 2 + 1 - c

    def plane(k, sign):
        dx, dy = OFFS[k]
        return ((x + sign * dx + 4) % 4) * 4 + (y + sign * dy + 4) % 4

    barrier = pltpu.get_barrier_semaphore()
    pl.semaphore_signal(barrier, inc=1, device_id=(gx, mate), device_id_type=MESH)
    for k in range(15):
        pl.semaphore_signal(barrier, inc=1, device_id=(plane(k, 1), gy), device_id_type=MESH)
    for d in range(1, 4):
        pl.semaphore_signal(barrier, inc=1, device_id=(gx, ((z + d) % 4) * 2 + c), device_id_type=MESH)

    for s in range(16):
        v = t_ref[s]
        h = v.astype(BF)
        hb[:, 128 * s:128 * s + 128] = h
        lb[:, 128 * s:128 * s + 128] = (v - h.astype(jnp.float32)).astype(BF)

    def dot(a, b):
        return lax.dot_general(a, b, NT, preferred_element_type=jnp.float32)

    for (r0, c0) in ((0, 0), (256, 0), (256, 256)):
        hr, lr = hb[r0:r0 + 256, :], lb[r0:r0 + 256, :]
        hc, lc = hb[c0:c0 + 256, :], lb[c0:c0 + 256, :]
        g = dot(hr, hc) + dot(hr, lc) + dot(lr, hc)
        for n, (i, j) in enumerate(BLOCKS):
            if r0 <= 128 * i < r0 + 256 and c0 <= 128 * j < c0 + 256:
                gp[16 * n:16 * n + 16] = g[128 * i - r0:128 * i - r0 + 128, 128 * j - c0:128 * j - c0 + 128].reshape(16, 8, 128)

    pl.semaphore_wait(barrier, 19)
    pieces = lambda core, g: pl.ds(80 * core + 5 * g, 5)

    def remote(src, dst, ss, rs, dev):
        return pltpu.make_async_remote_copy(src_ref=src, dst_ref=dst, send_sem=ss, recv_sem=rs, device_id=dev, device_id_type=MESH)

    A = [remote(gp.at[pieces(1 - c, plane(k, 1))], ra.at[k], sa.at[k], qa.at[k], (gx, mate)) for k in range(16)]
    for cp in A:
        cp.start()
    B = []
    for k in range(16):
        A[k].wait_recv()
        aa[k] = gp[pieces(c, plane(k, 1))] + ra[k]
        if k != SELF:
            cp = remote(aa.at[k], rb.at[k], sb.at[k], qb.at[k], (plane(k, 1), gy))
            cp.start()
            B.append(cp)
    total = aa[SELF]
    for k in range(14, -1, -1):
        B[k].wait_recv()
        total = total + rb[k]
    ab[...] = total
    rc[z] = total
    C = []
    for d in range(1, 4):
        cp = remote(ab, rc.at[z], sc.at[d], qc.at[d], (gx, ((z + d) % 4) * 2 + c))
        cp.start()
        C.append(cp)
    for cp in C:
        cp.wait_recv()
    total = (rc[0] + rc[1]) + (rc[2] + rc[3])
    ac[...] = total
    mine = pieces(c, gx)
    D = []
    for k in range(15):
        cp = remote(ac, o_ref.at[mine], sd.at[k], qd.at[k], (plane(k, 1), gy))
        cp.start()
        D.append(cp)
    o_ref[mine] = total
    E = [remote(ac, o_ref.at[mine], se.at[SELF], qe.at[SELF], (gx, mate))]
    E[0].start()
    for k in range(14, -1, -1):
        D[k].wait_recv()
        spot = pieces(c, plane(k, -1))
        cp = remote(o_ref.at[spot], o_ref.at[spot], se.at[k], qe.at[k], (gx, mate))
        cp.start()
        E.append(cp)
    for cp in E:
        cp.wait_recv()
    for cp in A + B + C + D + E:
        cp.wait_send()


def gram_sum(tensor):
    f = jnp.float32
    V, D = pltpu.VMEM, pltpu.SemaphoreType.DMA
    return pl.pallas_call(
        ar_kernel,
        out_shape=jax.ShapeDtypeStruct((160, 8, 128), f),
        in_specs=[pl.BlockSpec(memory_space=pltpu.VMEM)],
        out_specs=pl.BlockSpec(memory_space=pltpu.VMEM),
        scratch_shapes=[
            V((512, 2048), BF), V((512, 2048), BF),
            V((160, 8, 128), f), V((16, 5, 8, 128), f), V((16, 5, 8, 128), f), V((16, 5, 8, 128), f),
            V((5, 8, 128), f), V((4, 5, 8, 128), f), V((5, 8, 128), f),
            D((16,)), D((16,)), D((16,)), D((16,)), D((4,)), D((4,)), D((16,)), D((16,)), D((16,)), D((16,)),
        ],
        compiler_params=pltpu.CompilerParams(collective_id=0, has_side_effects=True, vmem_limit_bytes=28 << 20),
        name="gram_sum",
    )(tensor)


def split(x):
    h = x.astype(jnp.bfloat16)
    return h, (x - h.astype(jnp.float32)).astype(jnp.bfloat16)


def mm(a, b, ca=1, cb=0):
    ah, al = split(a)
    bh, bl = split(b)

    def dot(u, v):
        return lax.dot_general(u, v, (((ca,), (cb,)), ((), ())), preferred_element_type=jnp.float32)

    return dot(ah, bh) + (dot(ah, bl) + dot(al, bh))


LOOK = 2


def lanes(x, i):
    return jnp.broadcast_to(x[:, i:i + 1], (8, 128))


def rows(x, i):
    return jnp.broadcast_to(x[i:i + 1, :], (8, 128))


def chol_steps(A, one, li):
    row = lax.broadcasted_iota(jnp.int32, (8, 128), 0)
    lane = lax.broadcasted_iota(jnp.int32, (8, 128), 1)
    C = [lanes(A[0], j) * one for j in range(8)]
    for p in range(16):
        c = 8 * p
        done = (lane >= c) & (lane < c + 8)
        S = [[rows(C[j], i) for j in range(i + 1)] for i in range(8)]
        top = jnp.where(done, jnp.where(lane == row + c, 1.0, 0.0), A[p])
        V = [rows(top, i) for i in range(8)]
        near = range(p + 1, min(p + 1 + LOOK, 16))
        if p < 15:
            C = [lanes(A[p + 1], c + 8 + j) for j in range(8)]
        X = {g: [lanes(A[g], c + j) for j in range(8)] for g in range(p + 1, 16)}
        for g in range(p + 1, 16):
            A[g] = jnp.where(done, 0.0, A[g])
        L = [[None] * 8 for _ in range(8)]
        r = [None] * 8
        for j in range(8):
            r[j] = lax.rsqrt(S[j][j])
            for i in range(j + 1, 8):
                L[i][j] = S[i][j] * r[j]
            for i in range(j + 1, 8):
                for k in range(j + 1, i + 1):
                    S[i][k] = S[i][k] - L[i][j] * L[k][j]
            V[j] = V[j] * r[j]
            for g in near:
                x = X[g][j] * r[j]
                for k in range(j + 1, 8):
                    X[g][k] = X[g][k] - x * L[k][j]
                A[g] = A[g] - x * V[j]
                if g == p + 1:
                    for k in range(8):
                        C[k] = C[k] - x * rows(x, k)
            for i in range(j + 1, 8):
                V[i] = V[i] - L[i][j] * V[j]
        o = V[0]
        for i in range(1, 8):
            o = jnp.where(row == i, V[i], o)
        li[c:c + 8, :] = jnp.where(lane < c + 8, o, 0.0)
        yield
        if p + 1 + LOOK >= 16:
            continue
        F = list(V)
        for j in range(7, -1, -1):
            F[j] = F[j] * r[j]
            for i in range(j):
                F[i] = F[i] - L[j][i] * F[j]
        for g in range(p + 1 + LOOK, 16):
            t = [X[g][j] * F[j] for j in range(8)]
            t = [t[0] + t[1], t[2] + t[3], t[4] + t[5], t[6] + t[7]]
            A[g] = A[g] - ((t[0] + t[1]) + (t[2] + t[3]))


def groups(ref):
    return [ref[8 * g:8 * g + 8, :] for g in range(16)]


def run(*steps):
    steps = list(steps)
    while steps:
        for one in list(steps):
            if next(one, True) is True:
                steps.remove(one)


def sweeps_kernel(p_ref, b_ref, o_ref, g_ref, p, q, a, li, one_ref):
    n = 0
    for i in range(4):
        for j in range(i + 1):
            blk = p_ref[16 * n:16 * n + 16].reshape(128, 128)
            g_ref[128 * i:128 * i + 128, 128 * j:128 * j + 128] = blk
            if j < i:
                g_ref[128 * j:128 * j + 128, 128 * i:128 * i + 128] = blk.T
            n += 1
    one_ref[...] = jnp.ones((8, 128), jnp.float32)
    one = one_ref[...]
    first, second = 0, 3

    def product(s, k, source, cs):
        p[s + k] = mm(source, g_ref[...], cs, 0)
        for j in range(k + 1):
            a[s + j, k] = mm(p[s + j], p[s + k], 1, 1)

    def basis(s, k):
        q[s + k] = mm(li[s + k], p[s + k])

    def factor(s, k, j):
        a[s + k, j] = mm(li[s + k], a[s + k, j])

    def reduce_gram(s, k, i, j):
        a[s + i, j] -= mm(a[s + k, i], a[s + k, j], 0, 0)

    def reduce_product(s, k, j):
        p[s + j] -= mm(a[s + k, j], q[s + k], 0, 0)

    def chol(s, k):
        return chol_steps(groups(a.at[s + k, k]), one, li.at[s + k])

    for k in range(3):
        product(first, k, b_ref[:, 128 * k:128 * k + 128], 0)
    run(chol(first, 0))
    factor(first, 0, 1)
    reduce_gram(first, 0, 1, 1)
    basis(first, 0)
    product(second, 0, q[0], 1)
    factor(first, 0, 2)
    reduce_gram(first, 0, 1, 2)
    reduce_gram(first, 0, 2, 2)
    reduce_product(first, 0, 1)
    reduce_product(first, 0, 2)
    run(chol(first, 1), chol(second, 0))
    factor(first, 1, 2)
    reduce_gram(first, 1, 2, 2)
    basis(first, 1)
    product(second, 1, q[1], 1)
    factor(second, 0, 1)
    reduce_gram(second, 0, 1, 1)
    reduce_product(first, 1, 2)
    basis(second, 0)
    reduce_product(second, 0, 1)
    run(chol(first, 2), chol(second, 1))
    basis(first, 2)
    product(second, 2, q[2], 1)
    factor(second, 0, 2)
    reduce_gram(second, 0, 2, 2)
    factor(second, 1, 2)
    reduce_gram(second, 1, 2, 2)
    basis(second, 1)
    reduce_product(second, 0, 2)
    reduce_product(second, 1, 2)
    run(chol(second, 2))
    basis(second, 2)
    for k in range(3):
        o_ref[128 * k:128 * k + 128, :] = q[3 + k]


def sweeps(packed, start):
    f = jnp.float32
    whole = pl.BlockSpec(memory_space=pltpu.VMEM)
    return pl.pallas_call(
        sweeps_kernel,
        out_shape=jax.ShapeDtypeStruct((384, 512), f),
        in_specs=[whole] * 2, out_specs=whole,
        scratch_shapes=[pltpu.VMEM((512, 512), f), pltpu.VMEM((6, 128, 512), f), pltpu.VMEM((6, 128, 512), f),
                        pltpu.VMEM((6, 3, 128, 128), f), pltpu.VMEM((6, 128, 128), f), pltpu.VMEM((8, 128), f)],
        cost_estimate=pl.CostEstimate(flops=4000000000, bytes_accessed=3000000, transcendentals=0),
        compiler_params=pltpu.CompilerParams(vmem_limit_bytes=24 << 20), name="sweeps",
    )(packed, start)


RELS = [(2, 0), (2, 1), (1, 0), (3, 0), (1, 1), (3, 1), (0, 1)]
GROUPS = [(0, 4), (4, 16)]


def core_kernel(q_ref, t_ref, o_ref, qh, ql, y, ssem, rsem, osem):
    gx = lax.axis_index("gx")
    gy = lax.axis_index("gy")
    z, c = gy // 2, gy % 2

    def other(r):
        dz, dc = RELS[r]
        return ((z + dz) % 4) * 2 + (c + dc) % 2

    barrier = pltpu.get_barrier_semaphore()
    for r in range(7):
        pl.semaphore_signal(barrier, inc=1, device_id=(gx, other(r)), device_id_type=pl.DeviceIdType.MESH)
    v = q_ref[...]
    h = v.astype(jnp.bfloat16)
    qh[...] = h
    ql[...] = (v - h.astype(jnp.float32)).astype(jnp.bfloat16)

    def dot(a, b):
        return jnp.dot(a, b, preferred_element_type=jnp.float32)

    spot = pl.ds(pl.multiple_of(gy * 128, 128), 128)
    sends = []
    for n, (a, b) in enumerate(GROUPS):
        for k in range(a, b, 2):
            v = jnp.concatenate([t_ref[k], t_ref[k + 1]], axis=1)
            th = v.astype(jnp.bfloat16)
            tl = (v - th.astype(jnp.float32)).astype(jnp.bfloat16)
            out = dot(qh[...], th) + dot(qh[...], tl) + dot(ql[...], th)
            y[k] = out[:, :128]
            y[k + 1] = out[:, 128:]
        if n == 0:
            pl.semaphore_wait(barrier, 7)
        for r in range(7):
            cp = pltpu.make_async_remote_copy(
                src_ref=y.at[pl.ds(a, b - a), pl.ds(pl.multiple_of(48 * other(r), 8), 48)],
                dst_ref=o_ref.at[pl.ds(a, b - a), pl.ds(0, 48), spot],
                send_sem=ssem.at[r, n], recv_sem=rsem.at[r, n],
                device_id=(gx, other(r)), device_id_type=pl.DeviceIdType.MESH)
            cp.start()
            sends.append(cp)
    own = pltpu.make_async_copy(y.at[pl.ds(0, 16), pl.ds(pl.multiple_of(48 * gy, 8), 48)], o_ref.at[pl.ds(0, 16), pl.ds(0, 48), spot], osem)
    own.start()
    for cp in sends:
        cp.wait()
    own.wait()


def core_out(basis_t, tensor):
    f = jnp.float32
    V, D = pltpu.VMEM, pltpu.SemaphoreType.DMA
    ng = len(GROUPS)
    return pl.pallas_call(
        core_kernel,
        out_shape=jax.ShapeDtypeStruct((16, 48, 1024), f),
        in_specs=[pl.BlockSpec(memory_space=pltpu.VMEM), pl.BlockSpec(memory_space=pltpu.VMEM)],
        out_specs=pl.BlockSpec(memory_space=pltpu.VMEM),
        scratch_shapes=[V((384, 512), jnp.bfloat16), V((384, 512), jnp.bfloat16), V((16, 384, 128), f),
                        D((7, ng)), D((7, ng)), D],
        compiler_params=pltpu.CompilerParams(collective_id=1, has_side_effects=True, vmem_limit_bytes=20 << 20),
        name="core_out",
    )(basis_t, tensor)


def body(tensor, start_basis):
    return core_out(sweeps(gram_sum(tensor), start_basis), tensor)


def solution(mesh):
    placed = (P("gx", None, "gy"), P())
    return jax.shard_map(
        body, mesh=mesh, in_specs=placed, out_specs=P("gx", "gy", None), check_vma=False
    )
```
